32 devices in a mesh: pair: 2 (over core), lat: 4 (over y, x), tok: 4 (over z).
Axes of the slice: x: 2, y: 2, z: 4, core: 2. Of those that a mesh axis runs over, the one named last changes fastest.
Arguments:
- residual: bfloat16 [2, 512, 4096], P('pair', 'tok', 'lat'), may hold values from -6 to 6
- matches: int32 [2, 512], P('pair', 'tok'), may hold values from 0 to 511, as said below
- kl_grad: bfloat16 [512, 4096], P('tok', 'lat'), may hold values from -6 to 6
- active_blocks: int32 [64, 2], replicated, may hold values from 0 to 31, all different within a row; in each aligned block of 16 rows (0 to 15, 16 to 31, ...) at most 2 rows name the same one
- encoder: bfloat16 [4096, 4096], P(None, ('pair', 'lat', 'tok')), may hold values from -0.09375 to 0.09375
- encoder_offset_bias: float32 [4096], P(('pair', 'lat', 'tok')), may hold values from -3 to 3
- decoder: bfloat16 [4096, 4096], P(('pair', 'lat', 'tok')), may hold values from -0.5 to 0.5
- dec_bias: float32 [4096], P('lat'), may hold values from -3 to 3
Outputs:
- reconstruction: bfloat16 [512, 4096], P('tok', 'lat')
- scores: float32 [4096], P(('pair', 'lat', 'tok'))
The draws below stay inside these ranges and needn't reach their ends.
Inputs may be any that keep to these rules, and one draw needn't show every extreme that they name: For each model m and matched token k: k - 128 < matches[m, k] <= k (at least 0); where k is a positive multiple of 128, matches[m, k] = k - 127. `active_blocks`: each row lists 2 different latent blocks. Among the 16 rows of one tok index (aligned blocks of rows) no latent block is listed more than 2 times, and some latent block is listed exactly 2 times.
All inputs are finite; a program needn't handle non-finite values.
Results may differ from the reference program's by a relative error of at most 0.0085.
Values may be sent and summed in bfloat16 or wider, within the bound.
A program may use at most 64 MiB of HBM per device.

```python
import math
import jax
import jax.numpy as jnp
import numpy as np
from jax import lax

D = 4096
TOK_DEV = 128
TBLK = 8
LBLK = 128
MOST = 2
TOKENS = 512
TB_DEV = 16
TBLOCKS = 64
BLOCKS = 32
LATENTS = 4096
ACTIVE = 2


def draw_matches(key, part):
    lags = jax.random.randint(key, (2, TOKENS), 0, TOK_DEV)
    places = jnp.arange(TOKENS, dtype=jnp.int32)
    lags = jnp.where((places % TOK_DEV == 0)[None, :], TOK_DEV - 1, lags)
    return jnp.maximum(places[None, :] - lags, 0).astype(jnp.int32)


def level_of(stream_key, dims, shards, least, largest):
    level, own = 1.0, jax.random.fold_in(stream_key, 6)
    for dim, blocks in shards:
        steps = jnp.exp(jax.random.uniform(jax.random.fold_in(own, dim), (blocks,), jnp.float32, least / len(shards), largest / len(shards)))
        level = level * jnp.repeat(steps, dims[dim] // blocks).reshape([-1 if axis == dim else 1 for axis in range(len(dims))])
    return level


def routed_block(own_key, own, number, rows, count, top, limit, slope):
    order = jax.random.permutation(own_key, count)
    heavy_load, common = load_shares(count, rows * top, limit, slope, True), load_shares(count, rows * top, limit, slope, False)
    places = jnp.arange(count)

    def named(sizes, turn):
        used = int((sizes > 0).sum())
        fixed = max(1, used // 4)
        shifted = fixed + (places - fixed + turn * (used - fixed)) % max(1, count - fixed)
        return jnp.zeros((count,), jnp.int32).at[order[jnp.where(places < fixed, places, shifted)]].set(jnp.asarray(sizes, jnp.int32))

    sizes = jnp.where(number % 4 == 0, named(heavy_load, number // 4), named(common, number - number // 4 - 1))
    mixed = jax.random.permutation(jax.random.fold_in(own, 3), count)
    donor, receiver = mixed[0:count // 2 * 2:2], mixed[1:count // 2 * 2:2]
    room = jnp.minimum(sizes[donor] - 1, limit - sizes[receiver]) // 2
    room = jnp.where((donor == order[0]) | (receiver == order[0]) | (sizes[receiver] == 0), 0, jnp.maximum(room, 0))
    shifted = jax.random.randint(jax.random.fold_in(own, 4), (count // 2,), 0, 1 << 20) % (room + 1)
    sizes = sizes.at[donor].add(-shifted).at[receiver].add(shifted)
    items = jnp.searchsorted(jnp.cumsum(sizes), jnp.arange(rows * top), side="right").astype(jnp.int32)
    grid = items.reshape(top, rows).T
    grid = grid[jax.random.permutation(jax.random.fold_in(own, 1), rows)]
    turn = jax.random.randint(jax.random.fold_in(own, 2), (rows, 1), 0, top)
    return jnp.take_along_axis(grid, (jnp.arange(top)[None, :] + turn) % top, axis=1)


def load_shares(number_of, total, limit, slope, full):
    weights = [(1 << 20) // math.isqrt(standing ** slope) + 1 for standing in range(1, number_of + 1)]
    largest = limit if full else min(limit, max(-(-total // number_of), total * weights[0] // sum(weights)))
    least = 1 if total - largest >= number_of - 1 else 0
    given, surplus = [largest] + [least] * (number_of - 1), total - largest - least * (number_of - 1)
    while surplus > 0:
        free = [i for i in range(1, number_of) if given[i] < largest] or [i for i in range(1, number_of) if given[i] < limit]
        whole, budget = sum([weights[i] for i in free]), surplus
        for i in free:
            addition = min(limit - given[i], max(1, budget * weights[i] // whole), surplus)
            given[i] = given[i] + addition
            surplus = surplus - addition
    return np.array(given)


def centred(own_key, dims, width, bound, shards=(), held_as=jnp.bfloat16):
    values = width * jax.random.normal(own_key, dims, jnp.float32)
    if shards:
        values = values * level_of(own_key, dims, shards, -0.22, 0.18)
    return jnp.clip(values, -bound, bound).astype(held_as)


def setup_inputs(seed: int = 0) -> dict:
    streams_of = jax.random.split(jax.random.key(seed), 9)
    residual = centred(streams_of[0], (2, TOKENS, D), 1.0, 6.0, ((0, 2), (1, 4), (2, 4)))
    matches = draw_matches(jax.random.fold_in(streams_of[8], 71), 0)
    kl_grad = centred(streams_of[2], (TOKENS, D), 1.0, 6.0, ((0, 4), (1, 4)))
    active_blocks_keys = jax.random.split(jax.random.fold_in(streams_of[3], 1), TBLOCKS // TB_DEV)
    active_blocks_turns = jax.random.permutation(jax.random.fold_in(streams_of[3], 3), TBLOCKS // TB_DEV)
    active_blocks = jax.vmap(lambda own, number: routed_block(jax.random.fold_in(streams_of[3], 2), own, number, TB_DEV, BLOCKS, ACTIVE, MOST, 2))(active_blocks_keys, active_blocks_turns).reshape((TBLOCKS, ACTIVE))
    encoder = centred(streams_of[4], (D, LATENTS), D ** -0.5, 0.09375, ((1, 32),))
    encoder_offset_bias = centred(streams_of[5], (LATENTS,), 0.5, 3.0, ((0, 32),), jnp.float32)
    decoder = centred(streams_of[6], (LATENTS, D), (ACTIVE * LBLK // 2) ** -0.5, 0.5, ((0, 32),))
    dec_bias = centred(streams_of[7], (D,), 0.5, 3.0, ((0, 4),), jnp.float32)
    return {"residual": residual, "matches": matches, "kl_grad": kl_grad, "active_blocks": active_blocks, "encoder": encoder, "encoder_offset_bias": encoder_offset_bias, "decoder": decoder, "dec_bias": dec_bias}


def reference(residual, matches, kl_grad, active_blocks, encoder, encoder_offset_bias, decoder, dec_bias):
    base_rows = jnp.take(residual[0], matches[0], axis=0)
    chat_rows = jnp.take(residual[1], matches[1], axis=0)
    delta_rows = (chat_rows.astype(jnp.float32) - base_rows.astype(jnp.float32)).astype(jnp.bfloat16)
    enc_view = encoder.reshape(D, BLOCKS, LBLK)
    bias_view = encoder_offset_bias.reshape(BLOCKS, LBLK)
    dec_view = decoder.reshape(BLOCKS, LBLK, D)

    def one_block(inputs):
        input_rows, gradient_rows, listed = inputs
        encoder_selected = jnp.take(enc_view, listed, axis=1).astype(jnp.float32)
        decoder_selected = jnp.take(dec_view, listed, axis=0).astype(jnp.float32)
        preactivation = jnp.einsum('uz,znl->unl', input_rows.astype(jnp.float32), encoder_selected)
        preactivation = preactivation + jnp.take(bias_view, listed, axis=0)[None, :, :]
        activation_value = jnp.maximum(preactivation, 0.0)
        gradient_inner_product = jnp.einsum('wg,kug->wku', gradient_rows.astype(jnp.float32), decoder_selected)
        latent_credit = lax.optimization_barrier(jnp.sum(activation_value * gradient_inner_product, axis=0))
        padded_length = lax.optimization_barrier(activation_value.astype(jnp.bfloat16)).astype(jnp.float32)
        partial_results = jnp.einsum('esl,slj->sej', padded_length, decoder_selected).astype(jnp.bfloat16)
        partial_results = lax.optimization_barrier(partial_results).astype(jnp.float32)
        return (latent_credit, lax.optimization_barrier(jnp.sum(partial_results, axis=0)))
    block_credit, sums = lax.map(one_block, (delta_rows.reshape(TBLOCKS, TBLK, D), kl_grad.reshape(TBLOCKS, TBLK, D), active_blocks))
    scores = jnp.zeros((BLOCKS, LBLK), jnp.float32)
    scores = scores.at[active_blocks.reshape(-1)].add(block_credit.reshape(-1, LBLK))
    scores = (scores / math.sqrt(TOKENS / 8)).reshape(LATENTS)
    reconstruction = (sums.reshape(TOKENS, D) + dec_bias).astype(jnp.bfloat16)
    return (reconstruction, scores)
```

```python
import functools
import math

import jax
import jax.numpy as jnp
from jax import lax
from jax.experimental import pallas as pl
from jax.experimental.pallas import tpu as pltpu
from jax.sharding import PartitionSpec as P

TBLK = 8
MOST = 2


def passed_along(x, axis, by):
    devices = lax.axis_size(axis)
    pairs = [(i, i + by) for i in range(devices) if 0 <= i + by < devices]
    return lax.ppermute(x, axis, pairs)


def from_partner(x, axis, bit):
    return lax.ppermute(x, axis, [(i, i ^ 1 << bit) for i in range(lax.axis_size(axis))])


def slot_table(my_lists, targets, slot_ids):
    listed = jnp.any(my_lists[:, :, None] == targets[None, None, :], axis=1).astype(jnp.int32)
    ranking = jnp.cumsum(listed, axis=0) - listed
    return (listed.T[:, None, :] * (ranking.T[:, None, :] == slot_ids[None, :, None])).astype(
        jnp.bfloat16
    )


def shards(
    residual, matches, kl_grad, active_blocks, encoder, encoder_offset_bias, decoder, dec_bias
):
    tok_dev = residual.shape[1]
    tok_count = lax.axis_size("tok")
    lat_count = lax.axis_size("lat")
    tok_here = lax.axis_index("tok")
    own_rows = residual[0]
    earlier = passed_along(own_rows, "tok", 1)
    window = jnp.concatenate([earlier, own_rows], axis=0)
    first_row = (tok_here - 1) * tok_dev
    local_index = matches[0] - first_row
    matched = jnp.take(window, local_index, axis=0)
    partner = from_partner(matched, "pair", 0)
    is_chat = lax.axis_index("pair") == 1
    chat_rows = jnp.where(is_chat, matched, partner)
    base_rows = jnp.where(is_chat, partner, matched)
    delta_rows = (chat_rows.astype(jnp.float32) - base_rows.astype(jnp.float32)).astype(
        jnp.bfloat16
    )
    tb_dev = tok_dev // TBLK
    pair_base = lax.axis_index("pair") * lat_count
    row_base = (pair_base + lax.axis_index("lat")) * tok_count
    my_block = row_base + tok_here
    my_lists = lax.dynamic_slice_in_dim(active_blocks, tok_here * tb_dev, tb_dev, 0)
    slot_ids = jnp.arange(MOST, dtype=jnp.int32)
    targets = row_base + jnp.arange(tok_count, dtype=jnp.int32)
    chooser = slot_table(my_lists, targets, slot_ids)
    mine_listed = jnp.any(active_blocks == my_block, axis=1).astype(jnp.int32)
    counts = jnp.sum(mine_listed.reshape(tok_count, tb_dev), axis=1)
    padded_output = (slot_ids[None, :] < counts[:, None]).astype(jnp.float32)[:, :, None, None]

    def select_slots(blocks):
        return jnp.einsum(
            "ksb,btd->kstd", chooser, blocks, preferred_element_type=jnp.float32
        ).astype(jnp.bfloat16)

    full_delta, full_grad = (
        lax.all_gather(delta_rows, "lat", axis=1, tiled=True),
        lax.all_gather(kl_grad, "lat", axis=1, tiled=True),
    )
    full_width = full_delta.shape[1]
    sent_delta = select_slots(full_delta.reshape(tb_dev, TBLK, full_width))
    sent_grad = select_slots(full_grad.reshape(tb_dev, TBLK, full_width))
    got_delta, got_grad = (
        lax.all_to_all(sent_delta, "tok", split_axis=0, concat_axis=0, tiled=True),
        lax.all_to_all(sent_grad, "tok", split_axis=0, concat_axis=0, tiled=True),
    )
    preactivation = jnp.einsum(
        "kstd,dc->kstc", got_delta, encoder, preferred_element_type=jnp.float32
    )
    gradient_inner_product = jnp.einsum(
        "kstd,cd->kstc", got_grad, decoder, preferred_element_type=jnp.float32
    )
    activation_value = jnp.maximum(preactivation + encoder_offset_bias, 0.0) * padded_output
    every_token_rows = tok_dev * tok_count
    scores = jnp.sum(activation_value * gradient_inner_product, axis=(0, 1, 2)) / math.sqrt(
        every_token_rows / 8
    )
    activation_half_precision = activation_value.astype(jnp.bfloat16)
    pieces_out = jnp.einsum(
        "fazg,gh->fazh", activation_half_precision, decoder, preferred_element_type=jnp.float32
    ).astype(jnp.bfloat16)
    returned = lax.all_to_all(pieces_out, "tok", split_axis=0, concat_axis=0, tiled=True)
    source_sums = jnp.einsum(
        "ksb,kstd->btd", chooser, returned, preferred_element_type=jnp.float32
    ).reshape(tok_dev, -1)
    shared = lax.psum_scatter(
        source_sums.astype(jnp.bfloat16), "lat", scatter_dimension=1, tiled=True
    )
    summed = lax.psum(shared, "pair").astype(jnp.float32)
    return ((summed + dec_bias).astype(jnp.bfloat16), scores)


MESH = pl.DeviceIdType.MESH
F32 = jnp.float32
BF16 = jnp.bfloat16
SLOT_ROWS = MOST * TBLK


def remote(src, dst, send_sem, recv_sem, device):
    return pltpu.make_async_remote_copy(
        src_ref=src,
        dst_ref=dst,
        send_sem=send_sem,
        recv_sem=recv_sem,
        device_id=device,
        device_id_type=MESH,
    )


def kernel(
    PAIR,
    LAT,
    TOK,
    residual,
    matches,
    grad,
    act,
    encoder,
    enc_bias,
    decoder,
    dec_bias,
    out,
    scores,
    win,
    match_all,
    part_out,
    part_in,
    own_delta,
    delta_all,
    grad_all,
    choose,
    sent_delta,
    sent_grad,
    got_delta,
    got_grad,
    fire,
    pieces,
    back,
    sum_out,
    sum_in,
    enc_v,
    dec_v,
    local_sem,
    win_sem,
    match_send,
    match_recv,
    part_sem,
    delta_send,
    delta_recv,
    grad_send,
    grad_recv,
    sd_send,
    sd_recv,
    sg_send,
    sg_recv,
    pc_send,
    pc_recv,
    sum_send,
    sum_recv,
    out_sem,
):
    p = lax.axis_index("pair")
    l = lax.axis_index("lat")
    t = lax.axis_index("tok")
    rows, width = residual.shape
    half = width // PAIR
    group = PAIR * LAT
    j = p * LAT + l
    other = 1 - p
    tokens = rows * TOK
    has_left, has_right = t > 0, t < TOK - 1
    my_cols = pl.ds(pl.multiple_of(p * half, half), half)
    other_cols = pl.ds(pl.multiple_of(other * half, half), half)
    fc = l * PAIR + p

    peers = []
    for o in range(1, group):
        q = lax.rem(j + o, group)
        peers.append((q, q // LAT, lax.rem(q, LAT)))

    local = [
        pltpu.make_async_copy(residual.at[:, my_cols], win.at[p], local_sem.at[0]),
        pltpu.make_async_copy(grad.at[:, my_cols], grad_all.at[t], local_sem.at[1]),
        pltpu.make_async_copy(encoder, enc_v, local_sem.at[2]),
        pltpu.make_async_copy(decoder, dec_v, local_sem.at[3]),
    ]
    for copy in local:
        copy.start()

    barrier = pltpu.get_barrier_semaphore()
    for _, qp, ql in peers:
        pl.semaphore_signal(barrier, inc=1, device_id=(qp, ql, t), device_id_type=MESH)
    for there, where in ((has_left, t - 1), (has_right, t + 1)):
        @pl.when(there)
        def _():
            for c in range(PAIR):
                pl.semaphore_signal(barrier, inc=1, device_id=(c, l, where), device_id_type=MESH)
    sides = jnp.where(has_left, 1, 0) + jnp.where(has_right, 1, 0)
    pl.semaphore_wait(barrier, group - 1 + PAIR * sides)

    match_all[p * 2] = matches[...]
    m_partner = remote(
        matches, match_all.at[p * 2], match_send.at[0], match_recv.at[p, 0], (other, l, t)
    )
    m_partner.start()
    m_left = [
        remote(matches, match_all.at[p * 2 + 1], match_send.at[1 + c], match_recv.at[p, 1], (c, l, t - 1))
        for c in range(PAIR)
    ]

    @pl.when(has_left)
    def _():
        for copy in m_left:
            copy.start()

    w_copy = remote(residual.at[:, other_cols], win.at[p], win_sem.at[0], win_sem.at[1], (other, l, t))
    w_copy.start()

    g_right = remote(grad.at[:, my_cols], grad_all.at[t], grad_send.at[t, 0], grad_recv.at[t], (p, l, t + 1))
    g_left = remote(grad.at[:, my_cols], grad_all.at[t], grad_send.at[t, 1], grad_recv.at[t], (p, l, t - 1))

    @pl.when(has_right)
    def _():
        g_right.start()

    @pl.when(has_left)
    def _():
        g_left.start()

    n_sel = group * SLOT_ROWS
    r_id = lax.broadcasted_iota(jnp.int32, (n_sel, rows), 0)
    c_id = lax.broadcasted_iota(jnp.int32, (n_sel, rows), 1)
    block_of = (r_id // SLOT_ROWS) * TOK + t
    slot_of = lax.rem(r_id // TBLK, MOST).astype(F32)
    same_row = lax.rem(r_id, TBLK) == lax.rem(c_id, TBLK)
    u_r = lax.broadcasted_iota(jnp.int32, (rows, rows), 0)
    u_c = lax.broadcasted_iota(jnp.int32, (rows, rows), 1)
    before = jnp.where((u_r // TBLK < u_c // TBLK) & (lax.rem(u_r, TBLK) == 0), 1.0, 0.0).astype(BF16)
    for s in range(TOK):
        listed = jnp.zeros((n_sel, rows), F32)
        for a in range(act.shape[0]):
            listed = listed + jnp.where(act[a : a + 1, s * rows : (s + 1) * rows] == block_of, 1.0, 0.0)
        rank = jnp.dot(listed.astype(BF16), before, preferred_element_type=F32)
        choose[s] = jnp.where(same_row & (rank == slot_of), listed, 0.0).astype(BF16)

    m_recv = remote(matches, match_all.at[other * 2], match_send.at[0], match_recv.at[other, 0], (other, l, t))
    m_recv.wait_recv()
    local[0].wait()
    w_recv = remote(residual.at[:, other_cols], win.at[other], win_sem.at[0], win_sem.at[1], (other, l, t))
    w_recv.wait_recv()
    row_id = lax.broadcasted_iota(jnp.int32, (rows, rows), 0) + t * rows

    def matched(which):
        total = None
        for model, sign in ((0, -1.0), (1, 1.0)):
            hit = jnp.where(match_all[model * 2 + which] == row_id, sign, 0.0)
            term = jnp.dot(hit.T.astype(BF16), win[model], preferred_element_type=F32)
            total = term if total is None else total + term
        return total

    p_copy = remote(part_out, part_in, part_sem.at[0], part_sem.at[1], (p, l, t + 1))

    @pl.when(has_right)
    def _():
        for model in range(2):
            remote(
                matches, match_all.at[model * 2 + 1], match_send.at[0], match_recv.at[model, 1], (other, l, t)
            ).wait_recv()
        part_out[...] = matched(1).astype(BF16)
        p_copy.start()

    own_delta[...] = matched(0)

    @pl.when(has_left)
    def _():
        p_copy.wait_recv()
        own_delta[...] += part_in[...].astype(F32)

    delta_all[t] = own_delta[...].astype(BF16)

    def pass_on(buf, send, recv, s, i):
        right = remote(buf.at[s], buf.at[s], send.at[s, 0], recv.at[s], (p, l, t + 1))
        left = remote(buf.at[s], buf.at[s], send.at[s, 1], recv.at[s], (p, l, t - 1))
        return right, left

    def order(i):
        m = jnp.minimum(t, TOK - 1 - t)
        d = (i + 1) // 2
        near = jnp.where(lax.rem(i, 2) == 1, t - d, t + d)
        far = jnp.where(t < TOK - 1 - t, t + (i - m), t - (i - m))
        return jnp.where(i <= 2 * m, near, far)

    def spread(i, buf, send, recv, sent, got, s_send, s_recv, first):
        s = order(i)
        right, left = pass_on(buf, send, recv, s, i)

        @pl.when(i > 0)
        def _():
            right.wait_recv()

        own_goes = 0 if first else 1

        @pl.when(has_right & (s + own_goes <= t))
        def _():
            right.start()

        @pl.when(has_left & (s - own_goes >= t))
        def _():
            left.start()

        sent[s] = (
            jnp.dot(choose[s], buf[s], preferred_element_type=F32)
            .astype(BF16)
            .reshape(group, SLOT_ROWS, half)
        )
        for q, qp, ql in peers:
            remote(sent.at[s, q], got.at[fc, s], s_send.at[s, q], s_recv.at[fc, s], (qp, ql, t)).start()
        got[fc, s] = sent[s, j]

    def spread_delta(i, carry):
        spread(i, delta_all, delta_send, delta_recv, sent_delta, got_delta, sd_send, sd_recv, True)
        return carry

    def arrive(got, s_recv, s):
        for q, qp, ql in peers:
            qf = ql * PAIR + qp
            remote(got.at[qf, s], got.at[qf, s], s_recv.at[qf, s], s_recv.at[qf, s], (qp, ql, t)).wait_recv()

    def encode(i, carry):
        s = order(i)
        arrive(got_delta, sd_recv, s)
        pre = jnp.zeros((SLOT_ROWS, enc_v.shape[1]), F32)
        for c in range(group):
            pre = pre + jnp.dot(
                got_delta[c, s], enc_v[c * half : (c + 1) * half, :], preferred_element_type=F32
            )
        firing = jnp.maximum(pre + enc_bias[...], 0.0)
        fire[s] = firing
        lean = firing.astype(BF16)
        for c in range(group):
            pieces[s, c] = jnp.dot(
                lean, dec_v[:, c * half : (c + 1) * half], preferred_element_type=F32
            ).astype(BF16)
        for q, qp, ql in peers:
            remote(
                pieces.at[s, ql * PAIR + qp], back.at[s, j], pc_send.at[s, q], pc_recv.at[s, j], (qp, ql, t)
            ).start()
        back[s, j] = pieces[s, fc]
        return carry

    def spread_grad(i, carry):
        spread(i, grad_all, grad_send, grad_recv, sent_grad, got_grad, sg_send, sg_recv, False)
        return carry

    def first_loop(i, carry):
        spread_delta(i, 0)
        spread_grad(i, 0)
        return carry

    local[1].wait()
    lax.fori_loop(0, TOK, first_loop, 0)
    local[2].wait()
    local[3].wait()
    lax.fori_loop(0, TOK, encode, 0)

    def combine(k, carry):
        s = order(TOK - 1 - k)
        for q, qp, ql in peers:
            remote(back.at[s, q], back.at[s, q], pc_recv.at[s, q], pc_recv.at[s, q], (qp, ql, t)).wait_recv()
        put = choose[s].astype(F32).T.astype(BF16)
        own_delta[...] = jnp.dot(put, back[s].reshape(n_sel, half), preferred_element_type=F32)

        def add_from(side):
            remote(
                sum_out.at[s], sum_in.at[side, s], sum_send.at[s], sum_recv.at[side, s], (p, l, t)
            ).wait_recv()
            own_delta[...] += sum_in[side, s].astype(F32)

        @pl.when(has_left & (s >= t))
        def _():
            add_from(0)

        @pl.when(has_right & (s <= t))
        def _():
            add_from(1)

        @pl.when(s != t)
        def _():
            sum_out[s] = own_delta[...].astype(BF16)

        @pl.when(s > t)
        def _():
            remote(sum_out.at[s], sum_in.at[0, s], sum_send.at[s], sum_recv.at[0, s], (p, l, t + 1)).start()

        @pl.when(s < t)
        def _():
            remote(sum_out.at[s], sum_in.at[1, s], sum_send.at[s], sum_recv.at[1, s], (p, l, t - 1)).start()

        return carry

    lax.fori_loop(0, TOK, combine, 0)
    out[:, my_cols] = (own_delta[...] + dec_bias[:, my_cols]).astype(BF16)
    o_copy = remote(out.at[:, my_cols], out.at[:, my_cols], out_sem.at[0], out_sem.at[1], (other, l, t))
    o_copy.start()

    def arrive_grad(s, carry):
        arrive(got_grad, sg_recv, s)
        return carry

    lax.fori_loop(0, TOK, arrive_grad, 0)
    inner = jnp.zeros((TOK * SLOT_ROWS, enc_v.shape[1]), F32)
    for c in range(group):
        inner = inner + lax.dot_general(
            got_grad[c].reshape(TOK * SLOT_ROWS, half),
            dec_v[:, c * half : (c + 1) * half],
            (((1,), (1,)), ((), ())),
            preferred_element_type=F32,
        )
    total = jnp.zeros((1, enc_v.shape[1]), F32)
    heads = lax.rem(lax.broadcasted_iota(jnp.int32, (1, rows), 1), TBLK) == 0
    slot = (lax.broadcasted_iota(jnp.int32, (SLOT_ROWS, 1), 0) // TBLK).astype(F32)
    for s in range(TOK):
        mine = jnp.zeros((1, rows), F32)
        for a in range(act.shape[0]):
            mine = mine + jnp.where(act[a : a + 1, s * rows : (s + 1) * rows] == j * TOK + t, 1.0, 0.0)
        count = jnp.sum(jnp.where(heads, mine, 0.0), axis=1, keepdims=True)
        used = jnp.where(slot < count, fire[s], 0.0)
        total = total + jnp.sum(
            used * inner[s * SLOT_ROWS : (s + 1) * SLOT_ROWS], axis=0, keepdims=True
        )
    scores[...] = total / math.sqrt(tokens / TBLK)

    m_partner.wait_send()
    w_copy.wait_send()

    @pl.when(has_left)
    def _():
        for copy in m_left:
            copy.wait_send()

    @pl.when(has_right)
    def _():
        p_copy.wait_send()

    def drain(s, carry):
        for buf, send, recv in ((delta_all, delta_send, delta_recv), (grad_all, grad_send, grad_recv)):
            right, left = pass_on(buf, send, recv, s, 0)

            @pl.when(has_right & (s <= t))
            def _():
                right.wait_send()

            @pl.when(has_left & (s >= t))
            def _():
                left.wait_send()

        for q, qp, ql in peers:
            remote(sent_delta.at[s, q], got_delta.at[fc, s], sd_send.at[s, q], sd_recv.at[fc, s], (qp, ql, t)).wait_send()
            remote(sent_grad.at[s, q], got_grad.at[fc, s], sg_send.at[s, q], sg_recv.at[fc, s], (qp, ql, t)).wait_send()
            remote(pieces.at[s, q], back.at[s, j], pc_send.at[s, q], pc_recv.at[s, j], (qp, ql, t)).wait_send()

        @pl.when(s != t)
        def _():
            remote(sum_out.at[s], sum_in.at[0, s], sum_send.at[s], sum_recv.at[0, s], (p, l, t)).wait_send()

        return carry

    lax.fori_loop(0, TOK, drain, 0)
    o_copy.wait_send()
    remote(out.at[:, other_cols], out.at[:, other_cols], out_sem.at[0], out_sem.at[1], (other, l, t)).wait_recv()


def fused(
    residual, matches, kl_grad, active_blocks, encoder, encoder_offset_bias, decoder, dec_bias
):
    pair, lat, tok = (lax.axis_size(a) for a in ("pair", "lat", "tok"))
    _, rows, width = residual.shape
    half = width // pair
    group = pair * lat
    lats = encoder.shape[1]
    depth = encoder.shape[0]
    act = jnp.repeat(active_blocks.T, TBLK, axis=1)
    vmem = pl.BlockSpec(memory_space=pltpu.VMEM)
    hbm = pl.BlockSpec(memory_space=pl.ANY)
    dma = pltpu.SemaphoreType.DMA
    slots = (SLOT_ROWS, half)
    recon, scores = pl.pallas_call(
        functools.partial(kernel, pair, lat, tok),
        out_shape=(
            jax.ShapeDtypeStruct((rows, width), BF16),
            jax.ShapeDtypeStruct((1, lats), F32),
        ),
        in_specs=[hbm, vmem, hbm, vmem, hbm, vmem, hbm, vmem],
        out_specs=(vmem, vmem),
        scratch_shapes=[
            pltpu.VMEM((2, rows, half), BF16),
            pltpu.VMEM((4, 1, rows), jnp.int32),
            pltpu.VMEM((rows, half), BF16),
            pltpu.VMEM((rows, half), BF16),
            pltpu.VMEM((rows, half), F32),
            pltpu.VMEM((tok, rows, half), BF16),
            pltpu.VMEM((tok, rows, half), BF16),
            pltpu.VMEM((tok, group * SLOT_ROWS, rows), BF16),
            pltpu.VMEM((tok, group) + slots, BF16),
            pltpu.VMEM((tok, group) + slots, BF16),
            pltpu.VMEM((group, tok) + slots, BF16),
            pltpu.VMEM((group, tok) + slots, BF16),
            pltpu.VMEM((tok, SLOT_ROWS, lats), F32),
            pltpu.VMEM((tok, group) + slots, BF16),
            pltpu.VMEM((tok, group) + slots, BF16),
            pltpu.VMEM((tok, rows, half), BF16),
            pltpu.VMEM((2, tok, rows, half), BF16),
            pltpu.VMEM((depth, lats), BF16),
            pltpu.VMEM((lats, depth), BF16),
            dma((4,)),
            dma((2,)),
            dma((3,)),
            dma((2, 2)),
            dma((2,)),
            dma((tok, 2)),
            dma((tok,)),
            dma((tok, 2)),
            dma((tok,)),
            dma((tok, group)),
            dma((group, tok)),
            dma((tok, group)),
            dma((group, tok)),
            dma((tok, group)),
            dma((tok, group)),
            dma((tok,)),
            dma((2, tok)),
            dma((2,)),
        ],
        compiler_params=pltpu.CompilerParams(
            collective_id=0, has_side_effects=True, vmem_limit_bytes=40 * 1024 * 1024
        ),
    )(
        residual[0],
        matches,
        kl_grad,
        act,
        encoder,
        encoder_offset_bias[None],
        decoder,
        dec_bias[None],
    )
    return recon, scores[0]


def solution(mesh):
    placed = (
        P("pair", "tok", "lat"),
        P("pair", "tok"),
        P("tok", "lat"),
        P(),
        P(None, ("pair", "lat", "tok")),
        P(("pair", "lat", "tok")),
        P(("pair", "lat", "tok"), None),
        P("lat"),
    )


    def body(*args):
        residual = args[0]
        half = residual.shape[2] // mesh.shape["pair"]
        fits = mesh.shape["pair"] == 2 and residual.shape[2] % 2 == 0 and half % 128 == 0
        return (fused if fits else shards)(*args)

    return jax.shard_map(
        body,
        mesh=mesh,
        in_specs=placed,
        out_specs=(P("tok", "lat"), P(("pair", "lat", "tok"))),
        check_vma=False,
    )
```

```python
import functools
import math

import jax
import jax.numpy as jnp
from jax import lax
from jax.experimental import pallas as pl
from jax.experimental.pallas import tpu as pltpu
from jax.sharding import PartitionSpec as P

TBLK = 8
MOST = 2


def passed_along(x, axis, by):
    devices = lax.axis_size(axis)
    pairs = [(i, i + by) for i in range(devices) if 0 <= i + by < devices]
    return lax.ppermute(x, axis, pairs)


def from_partner(x, axis, bit):
    return lax.ppermute(x, axis, [(i, i ^ 1 << bit) for i in range(lax.axis_size(axis))])


def slot_table(my_lists, targets, slot_ids):
    listed = jnp.any(my_lists[:, :, None] == targets[None, None, :], axis=1).astype(jnp.int32)
    ranking = jnp.cumsum(listed, axis=0) - listed
    return (listed.T[:, None, :] * (ranking.T[:, None, :] == slot_ids[None, :, None])).astype(
        jnp.bfloat16
    )


def shards(
    residual, matches, kl_grad, active_blocks, encoder, encoder_offset_bias, decoder, dec_bias
):
    tok_dev = residual.shape[1]
    tok_count = lax.axis_size("tok")
    lat_count = lax.axis_size("lat")
    tok_here = lax.axis_index("tok")
    own_rows = residual[0]
    earlier = passed_along(own_rows, "tok", 1)
    window = jnp.concatenate([earlier, own_rows], axis=0)
    first_row = (tok_here - 1) * tok_dev
    local_index = matches[0] - first_row
    matched = jnp.take(window, local_index, axis=0)
    partner = from_partner(matched, "pair", 0)
    is_chat = lax.axis_index("pair") == 1
    chat_rows = jnp.where(is_chat, matched, partner)
    base_rows = jnp.where(is_chat, partner, matched)
    delta_rows = (chat_rows.astype(jnp.float32) - base_rows.astype(jnp.float32)).astype(
        jnp.bfloat16
    )
    tb_dev = tok_dev // TBLK
    pair_base = lax.axis_index("pair") * lat_count
    row_base = (pair_base + lax.axis_index("lat")) * tok_count
    my_block = row_base + tok_here
    my_lists = lax.dynamic_slice_in_dim(active_blocks, tok_here * tb_dev, tb_dev, 0)
    slot_ids = jnp.arange(MOST, dtype=jnp.int32)
    targets = row_base + jnp.arange(tok_count, dtype=jnp.int32)
    chooser = slot_table(my_lists, targets, slot_ids)
    mine_listed = jnp.any(active_blocks == my_block, axis=1).astype(jnp.int32)
    counts = jnp.sum(mine_listed.reshape(tok_count, tb_dev), axis=1)
    padded_output = (slot_ids[None, :] < counts[:, None]).astype(jnp.float32)[:, :, None, None]

    def select_slots(blocks):
        return jnp.einsum(
            "ksb,btd->kstd", chooser, blocks, preferred_element_type=jnp.float32
        ).astype(jnp.bfloat16)

    full_delta, full_grad = (
        lax.all_gather(delta_rows, "lat", axis=1, tiled=True),
        lax.all_gather(kl_grad, "lat", axis=1, tiled=True),
    )
    full_width = full_delta.shape[1]
    sent_delta = select_slots(full_delta.reshape(tb_dev, TBLK, full_width))
    sent_grad = select_slots(full_grad.reshape(tb_dev, TBLK, full_width))
    got_delta, got_grad = (
        lax.all_to_all(sent_delta, "tok", split_axis=0, concat_axis=0, tiled=True),
        lax.all_to_all(sent_grad, "tok", split_axis=0, concat_axis=0, tiled=True),
    )
    preactivation = jnp.einsum(
        "kstd,dc->kstc", got_delta, encoder, preferred_element_type=jnp.float32
    )
    gradient_inner_product = jnp.einsum(
        "kstd,cd->kstc", got_grad, decoder, preferred_element_type=jnp.float32
    )
    activation_value = jnp.maximum(preactivation + encoder_offset_bias, 0.0) * padded_output
    every_token_rows = tok_dev * tok_count
    scores = jnp.sum(activation_value * gradient_inner_product, axis=(0, 1, 2)) / math.sqrt(
        every_token_rows / 8
    )
    activation_half_precision = activation_value.astype(jnp.bfloat16)
    pieces_out = jnp.einsum(
        "fazg,gh->fazh", activation_half_precision, decoder, preferred_element_type=jnp.float32
    ).astype(jnp.bfloat16)
    returned = lax.all_to_all(pieces_out, "tok", split_axis=0, concat_axis=0, tiled=True)
    source_sums = jnp.einsum(
        "ksb,kstd->btd", chooser, returned, preferred_element_type=jnp.float32
    ).reshape(tok_dev, -1)
    shared = lax.psum_scatter(
        source_sums.astype(jnp.bfloat16), "lat", scatter_dimension=1, tiled=True
    )
    summed = lax.psum(shared, "pair").astype(jnp.float32)
    return ((summed + dec_bias).astype(jnp.bfloat16), scores)


MESH = pl.DeviceIdType.MESH
F32 = jnp.float32
BF16 = jnp.bfloat16
SLOT_ROWS = MOST * TBLK


def remote(src, dst, send_sem, recv_sem, device):
    return pltpu.make_async_remote_copy(
        src_ref=src,
        dst_ref=dst,
        send_sem=send_sem,
        recv_sem=recv_sem,
        device_id=device,
        device_id_type=MESH,
    )


def kernel(
    PAIR,
    LAT,
    TOK,
    residual,
    matches,
    grad,
    act,
    encoder,
    enc_bias,
    decoder,
    dec_bias,
    out,
    scores,
    win,
    match_all,
    part_out,
    part_in,
    own_delta,
    delta_all,
    grad_all,
    choose,
    put,
    sent_delta,
    sent_grad,
    got_delta,
    got_grad,
    fire,
    pieces,
    back,
    sum_out,
    sum_in,
    enc_v,
    dec_v,
    local_sem,
    win_sem,
    match_send,
    match_recv,
    part_sem,
    delta_send,
    delta_recv,
    grad_send,
    grad_recv,
    sd_send,
    sd_recv,
    sg_send,
    sg_recv,
    pc_send,
    pc_recv,
    sum_send,
    sum_recv,
    out_sem,
):
    p = lax.axis_index("pair")
    l = lax.axis_index("lat")
    t = lax.axis_index("tok")
    rows, width = residual.shape
    half = width // PAIR
    group = PAIR * LAT
    j = p * LAT + l
    other = 1 - p
    tokens = rows * TOK
    has_left, has_right = t > 0, t < TOK - 1
    my_cols = pl.ds(pl.multiple_of(p * half, half), half)
    other_cols = pl.ds(pl.multiple_of(other * half, half), half)
    fc = l * PAIR + p

    peers = []
    for o in range(1, group):
        q = lax.rem(j + o, group)
        peers.append((q, q // LAT, lax.rem(q, LAT)))

    local = [
        pltpu.make_async_copy(residual.at[:, my_cols], win.at[p], local_sem.at[0]),
        pltpu.make_async_copy(grad.at[:, my_cols], grad_all.at[t], local_sem.at[1]),
        pltpu.make_async_copy(encoder, enc_v, local_sem.at[2]),
        pltpu.make_async_copy(decoder, dec_v, local_sem.at[3]),
    ]
    for copy in local:
        copy.start()

    barrier = pltpu.get_barrier_semaphore()
    for _, qp, ql in peers:
        pl.semaphore_signal(barrier, inc=1, device_id=(qp, ql, t), device_id_type=MESH)
    for where in range(TOK):
        @pl.when(t != where)
        def _():
            pl.semaphore_signal(barrier, inc=1, device_id=(p, l, where), device_id_type=MESH)

        @pl.when((where == t - 1) | (where == t + 1))
        def _():
            pl.semaphore_signal(barrier, inc=1, device_id=(other, l, where), device_id_type=MESH)
    n_sel = group * SLOT_ROWS
    r_id = lax.broadcasted_iota(jnp.int32, (n_sel, rows), 0)
    c_id = lax.broadcasted_iota(jnp.int32, (n_sel, rows), 1)
    block_of = (r_id // SLOT_ROWS) * TOK + t
    slot_of = lax.rem(r_id // TBLK, MOST).astype(F32)
    same_row = lax.rem(r_id, TBLK) == lax.rem(c_id, TBLK)
    u_r = lax.broadcasted_iota(jnp.int32, (rows, rows), 0)
    u_c = lax.broadcasted_iota(jnp.int32, (rows, rows), 1)
    before = jnp.where((u_r // TBLK < u_c // TBLK) & (lax.rem(u_r, TBLK) == 0), 1.0, 0.0).astype(BF16)
    for s in range(TOK):
        listed = jnp.zeros((n_sel, rows), F32)
        for a in range(act.shape[0]):
            listed = listed + jnp.where(act[a : a + 1, s * rows : (s + 1) * rows] == block_of, 1.0, 0.0)
        rank = jnp.dot(listed.astype(BF16), before, preferred_element_type=F32)
        chosen = jnp.where(same_row & (rank == slot_of), listed, 0.0)
        choose[s] = chosen.astype(BF16)
        put[s] = chosen.T.astype(BF16)

    sides = jnp.where(has_left, 1, 0) + jnp.where(has_right, 1, 0)
    pl.semaphore_wait(barrier, group - 1 + TOK - 1 + sides)

    match_all[p * 2] = matches[...]
    m_partner = remote(
        matches, match_all.at[p * 2], match_send.at[0], match_recv.at[p, 0], (other, l, t)
    )
    m_partner.start()
    m_left = [
        remote(matches, match_all.at[p * 2 + 1], match_send.at[1 + c], match_recv.at[p, 1], (c, l, t - 1))
        for c in range(PAIR)
    ]

    @pl.when(has_left)
    def _():
        for copy in m_left:
            copy.start()

    w_copy = remote(residual.at[:, other_cols], win.at[p], win_sem.at[0], win_sem.at[1], (other, l, t))
    w_copy.start()

    g_right = remote(grad.at[:, my_cols], grad_all.at[t], grad_send.at[t, 0], grad_recv.at[t], (p, l, t + 1))
    g_left = remote(grad.at[:, my_cols], grad_all.at[t], grad_send.at[t, 1], grad_recv.at[t], (p, l, t - 1))

    @pl.when(has_right)
    def _():
        g_right.start()

    @pl.when(has_left)
    def _():
        g_left.start()

    def pass_on(buf, send, recv, s):
        right = remote(buf.at[s], buf.at[s], send.at[s, 0], recv.at[s], (p, l, t + 1))
        left = remote(buf.at[s], buf.at[s], send.at[s, 1], recv.at[s], (p, l, t - 1))
        return right, left

    def order(i):
        m = jnp.minimum(t, TOK - 1 - t)
        d = (i + 1) // 2
        near = jnp.where(lax.rem(i, 2) == 1, t - d, t + d)
        far = jnp.where(t < TOK - 1 - t, t + (i - m), t - (i - m))
        return jnp.where(i <= 2 * m, near, far)

    def spread(i, buf, send, recv, sent, got, s_send, s_recv, first):
        s = order(i)
        right, left = pass_on(buf, send, recv, s)

        @pl.when(s != t)
        def _():
            right.wait_recv()

        own_goes = 0 if first else 1

        @pl.when(has_right & (s + own_goes <= t))
        def _():
            right.start()

        @pl.when(has_left & (s - own_goes >= t))
        def _():
            left.start()

        sent[s] = (
            jnp.dot(choose[s], buf[s], preferred_element_type=F32)
            .astype(BF16)
            .reshape(group, SLOT_ROWS, half)
        )
        for q, qp, ql in peers:
            remote(sent.at[s, q], got.at[fc, s], s_send.at[s, q], s_recv.at[fc, s], (qp, ql, t)).start()
        got[fc, s] = sent[s, j]

    def spread_delta(i):
        spread(i, delta_all, delta_send, delta_recv, sent_delta, got_delta, sd_send, sd_recv, True)

    def arrive(got, s_recv, s):
        for q, qp, ql in peers:
            qf = ql * PAIR + qp
            remote(got.at[qf, s], got.at[qf, s], s_recv.at[qf, s], s_recv.at[qf, s], (qp, ql, t)).wait_recv()

    def encode(i):
        s = order(i)
        arrive(got_delta, sd_recv, s)
        pre = jnp.zeros((SLOT_ROWS, enc_v.shape[1]), F32)
        for c in range(group):
            pre = pre + jnp.dot(
                got_delta[c, s], enc_v[c * half : (c + 1) * half, :], preferred_element_type=F32
            )
        firing = jnp.maximum(pre + enc_bias[...], 0.0)
        fire[s] = firing
        lean = firing.astype(BF16)
        for c in range(group):
            pieces[s, c] = jnp.dot(
                lean, dec_v[:, c * half : (c + 1) * half], preferred_element_type=F32
            ).astype(BF16)
        for q, qp, ql in peers:
            remote(
                pieces.at[s, ql * PAIR + qp], back.at[s, j], pc_send.at[s, q], pc_recv.at[s, j], (qp, ql, t)
            ).start()
        back[s, j] = pieces[s, fc]

    def spread_grad(i):
        spread(i, grad_all, grad_send, grad_recv, sent_grad, got_grad, sg_send, sg_recv, False)

    local[1].wait()
    spread_grad(0)
    m_recv = remote(matches, match_all.at[other * 2], match_send.at[0], match_recv.at[other, 0], (other, l, t))
    m_recv.wait_recv()
    local[0].wait()
    w_recv = remote(residual.at[:, other_cols], win.at[other], win_sem.at[0], win_sem.at[1], (other, l, t))
    w_recv.wait_recv()
    row_id = lax.broadcasted_iota(jnp.int32, (rows, rows), 0) + t * rows

    def matched(which):
        total = None
        for model, sign in ((0, -1.0), (1, 1.0)):
            hit = jnp.where(match_all[model * 2 + which] == row_id, sign, 0.0)
            term = jnp.dot(hit.T.astype(BF16), win[model], preferred_element_type=F32)
            total = term if total is None else total + term
        return total

    p_copy = remote(part_out, part_in, part_sem.at[0], part_sem.at[1], (p, l, t + 1))

    @pl.when(has_right)
    def _():
        for model in range(2):
            remote(
                matches, match_all.at[model * 2 + 1], match_send.at[0], match_recv.at[model, 1], (other, l, t)
            ).wait_recv()
        part_out[...] = matched(1).astype(BF16)
        p_copy.start()

    own_delta[...] = matched(0)
    if TOK > 1:
        spread_grad(1)

    @pl.when(has_left)
    def _():
        p_copy.wait_recv()
        own_delta[...] += part_in[...].astype(F32)

    delta_all[t] = own_delta[...].astype(BF16)

    def place(i):
        s = order(i)
        for q, qp, ql in peers:
            remote(back.at[s, q], back.at[s, q], pc_recv.at[s, q], pc_recv.at[s, q], (qp, ql, t)).wait_recv()
        placed = jnp.dot(put[s], back[s].reshape(n_sel, half), preferred_element_type=F32)

        @pl.when(s == t)
        def _():
            own_delta[...] = placed

        @pl.when(s != t)
        def _():
            sum_out[s] = placed.astype(BF16)
            remote(sum_out.at[s], sum_in.at[t], sum_send.at[s], sum_recv.at[t], (p, l, s)).start()

    spread_delta(0)
    local[2].wait()
    local[3].wait()

    def step(i, carry):
        encode(i)

        @pl.when(i + 1 < TOK)
        def _():
            spread_delta(i + 1)

        place(i)

        @pl.when(i + 2 < TOK)
        def _():
            spread_grad(i + 2)

        return carry

    lax.fori_loop(0, TOK - 1, step, 0)
    encode(TOK - 1)

    def arrive_grad(s, carry):
        arrive(got_grad, sg_recv, s)
        return carry

    lax.fori_loop(0, TOK, arrive_grad, 0)
    inner = jnp.zeros((TOK * SLOT_ROWS, enc_v.shape[1]), F32)
    for c in range(group):
        inner = inner + lax.dot_general(
            got_grad[c].reshape(TOK * SLOT_ROWS, half),
            dec_v[:, c * half : (c + 1) * half],
            (((1,), (1,)), ((), ())),
            preferred_element_type=F32,
        )
    place(TOK - 1)

    total = jnp.zeros((1, enc_v.shape[1]), F32)
    heads = lax.rem(lax.broadcasted_iota(jnp.int32, (1, rows), 1), TBLK) == 0
    slot = (lax.broadcasted_iota(jnp.int32, (SLOT_ROWS, 1), 0) // TBLK).astype(F32)
    for s in range(TOK):
        mine = jnp.zeros((1, rows), F32)
        for a in range(act.shape[0]):
            mine = mine + jnp.where(act[a : a + 1, s * rows : (s + 1) * rows] == j * TOK + t, 1.0, 0.0)
        count = jnp.sum(jnp.where(heads, mine, 0.0), axis=1, keepdims=True)
        used = jnp.where(slot < count, fire[s], 0.0)
        total = total + jnp.sum(
            used * inner[s * SLOT_ROWS : (s + 1) * SLOT_ROWS], axis=0, keepdims=True
        )
    scores[...] = total / math.sqrt(tokens / TBLK)

    for i in range(1, TOK):
        s = order(i)
        remote(sum_out.at[s], sum_in.at[s], sum_send.at[s], sum_recv.at[s], (p, l, s)).wait_recv()
        own_delta[...] += sum_in[s].astype(F32)

    out[:, my_cols] = (own_delta[...] + dec_bias[:, my_cols]).astype(BF16)
    o_copy = remote(out.at[:, my_cols], out.at[:, my_cols], out_sem.at[0], out_sem.at[1], (other, l, t))
    o_copy.start()

    m_partner.wait_send()
    w_copy.wait_send()

    @pl.when(has_left)
    def _():
        for copy in m_left:
            copy.wait_send()

    @pl.when(has_right)
    def _():
        p_copy.wait_send()

    def drain(s, carry):
        for buf, send, recv in ((delta_all, delta_send, delta_recv), (grad_all, grad_send, grad_recv)):
            right, left = pass_on(buf, send, recv, s)

            @pl.when(has_right & (s <= t))
            def _():
                right.wait_send()

            @pl.when(has_left & (s >= t))
            def _():
                left.wait_send()

        for q, qp, ql in peers:
            remote(sent_delta.at[s, q], got_delta.at[fc, s], sd_send.at[s, q], sd_recv.at[fc, s], (qp, ql, t)).wait_send()
            remote(sent_grad.at[s, q], got_grad.at[fc, s], sg_send.at[s, q], sg_recv.at[fc, s], (qp, ql, t)).wait_send()
            remote(pieces.at[s, q], back.at[s, j], pc_send.at[s, q], pc_recv.at[s, j], (qp, ql, t)).wait_send()

        @pl.when(s != t)
        def _():
            remote(sum_out.at[s], sum_in.at[t], sum_send.at[s], sum_recv.at[t], (p, l, s)).wait_send()

        return carry

    lax.fori_loop(0, TOK, drain, 0)
    o_copy.wait_send()
    remote(out.at[:, other_cols], out.at[:, other_cols], out_sem.at[0], out_sem.at[1], (other, l, t)).wait_recv()


def fused(
    residual, matches, kl_grad, active_blocks, encoder, encoder_offset_bias, decoder, dec_bias
):
    pair, lat, tok = (lax.axis_size(a) for a in ("pair", "lat", "tok"))
    _, rows, width = residual.shape
    half = width // pair
    group = pair * lat
    lats = encoder.shape[1]
    depth = encoder.shape[0]
    act = jnp.repeat(active_blocks.T, TBLK, axis=1)
    vmem = pl.BlockSpec(memory_space=pltpu.VMEM)
    hbm = pl.BlockSpec(memory_space=pltpu.HBM)
    dma = pltpu.SemaphoreType.DMA
    slots = (SLOT_ROWS, half)
    recon, scores = pl.pallas_call(
        functools.partial(kernel, pair, lat, tok),
        out_shape=(
            jax.ShapeDtypeStruct((rows, width), BF16),
            jax.ShapeDtypeStruct((1, lats), F32),
        ),
        in_specs=[hbm, vmem, hbm, vmem, hbm, vmem, hbm, vmem],
        out_specs=(vmem, vmem),
        scratch_shapes=[
            pltpu.VMEM((2, rows, half), BF16),
            pltpu.VMEM((4, 1, rows), jnp.int32),
            pltpu.VMEM((rows, half), BF16),
            pltpu.VMEM((rows, half), BF16),
            pltpu.VMEM((rows, half), F32),
            pltpu.VMEM((tok, rows, half), BF16),
            pltpu.VMEM((tok, rows, half), BF16),
            pltpu.VMEM((tok, group * SLOT_ROWS, rows), BF16),
            pltpu.VMEM((tok, rows, group * SLOT_ROWS), BF16),
            pltpu.VMEM((tok, group) + slots, BF16),
            pltpu.VMEM((tok, group) + slots, BF16),
            pltpu.VMEM((group, tok) + slots, BF16),
            pltpu.VMEM((group, tok) + slots, BF16),
            pltpu.VMEM((tok, SLOT_ROWS, lats), F32),
            pltpu.VMEM((tok, group) + slots, BF16),
            pltpu.VMEM((tok, group) + slots, BF16),
            pltpu.VMEM((tok, rows, half), BF16),
            pltpu.VMEM((tok, rows, half), BF16),
            pltpu.VMEM((depth, lats), BF16),
            pltpu.VMEM((lats, depth), BF16),
            dma((4,)),
            dma((2,)),
            dma((3,)),
            dma((2, 2)),
            dma((2,)),
            dma((tok, 2)),
            dma((tok,)),
            dma((tok, 2)),
            dma((tok,)),
            dma((tok, group)),
            dma((group, tok)),
            dma((tok, group)),
            dma((group, tok)),
            dma((tok, group)),
            dma((tok, group)),
            dma((tok,)),
            dma((tok,)),
            dma((2,)),
        ],
        compiler_params=pltpu.CompilerParams(
            collective_id=0, has_side_effects=True, vmem_limit_bytes=40 * 1024 * 1024
        ),
    )(
        residual[0],
        matches,
        kl_grad,
        act,
        encoder,
        encoder_offset_bias[None],
        decoder,
        dec_bias[None],
    )
    return recon, scores[0]


def solution(mesh):
    placed = (
        P("pair", "tok", "lat"),
        P("pair", "tok"),
        P("tok", "lat"),
        P(),
        P(None, ("pair", "lat", "tok")),
        P(("pair", "lat", "tok")),
        P(("pair", "lat", "tok"), None),
        P("lat"),
    )


    def body(*args):
        residual = args[0]
        half = residual.shape[2] // mesh.shape["pair"]
        fits = mesh.shape["pair"] == 2 and residual.shape[2] % 2 == 0 and half % 128 == 0
        return (fused if fits else shards)(*args)

    return jax.shard_map(
        body,
        mesh=mesh,
        in_specs=placed,
        out_specs=(P("tok", "lat"), P(("pair", "lat", "tok"))),
        check_vma=False,
    )
```

```python
import functools
import math

import jax
import jax.numpy as jnp
from jax import lax
from jax.experimental import pallas as pl
from jax.experimental.pallas import tpu as pltpu
from jax.sharding import PartitionSpec as P

TBLK = 8
MOST = 2


def passed_along(x, axis, by):
    devices = lax.axis_size(axis)
    pairs = [(i, i + by) for i in range(devices) if 0 <= i + by < devices]
    return lax.ppermute(x, axis, pairs)


def from_partner(x, axis, bit):
    return lax.ppermute(x, axis, [(i, i ^ 1 << bit) for i in range(lax.axis_size(axis))])


def slot_table(my_lists, targets, slot_ids):
    listed = jnp.any(my_lists[:, :, None] == targets[None, None, :], axis=1).astype(jnp.int32)
    ranking = jnp.cumsum(listed, axis=0) - listed
    return (listed.T[:, None, :] * (ranking.T[:, None, :] == slot_ids[None, :, None])).astype(
        jnp.bfloat16
    )


def shards(
    residual, matches, kl_grad, active_blocks, encoder, encoder_offset_bias, decoder, dec_bias
):
    tok_dev = residual.shape[1]
    tok_count = lax.axis_size("tok")
    lat_count = lax.axis_size("lat")
    tok_here = lax.axis_index("tok")
    own_rows = residual[0]
    earlier = passed_along(own_rows, "tok", 1)
    window = jnp.concatenate([earlier, own_rows], axis=0)
    first_row = (tok_here - 1) * tok_dev
    local_index = matches[0] - first_row
    matched = jnp.take(window, local_index, axis=0)
    partner = from_partner(matched, "pair", 0)
    is_chat = lax.axis_index("pair") == 1
    chat_rows = jnp.where(is_chat, matched, partner)
    base_rows = jnp.where(is_chat, partner, matched)
    delta_rows = (chat_rows.astype(jnp.float32) - base_rows.astype(jnp.float32)).astype(
        jnp.bfloat16
    )
    tb_dev = tok_dev // TBLK
    pair_base = lax.axis_index("pair") * lat_count
    row_base = (pair_base + lax.axis_index("lat")) * tok_count
    my_block = row_base + tok_here
    my_lists = lax.dynamic_slice_in_dim(active_blocks, tok_here * tb_dev, tb_dev, 0)
    slot_ids = jnp.arange(MOST, dtype=jnp.int32)
    targets = row_base + jnp.arange(tok_count, dtype=jnp.int32)
    chooser = slot_table(my_lists, targets, slot_ids)
    mine_listed = jnp.any(active_blocks == my_block, axis=1).astype(jnp.int32)
    counts = jnp.sum(mine_listed.reshape(tok_count, tb_dev), axis=1)
    padded_output = (slot_ids[None, :] < counts[:, None]).astype(jnp.float32)[:, :, None, None]

    def select_slots(blocks):
        return jnp.einsum(
            "ksb,btd->kstd", chooser, blocks, preferred_element_type=jnp.float32
        ).astype(jnp.bfloat16)

    full_delta, full_grad = (
        lax.all_gather(delta_rows, "lat", axis=1, tiled=True),
        lax.all_gather(kl_grad, "lat", axis=1, tiled=True),
    )
    full_width = full_delta.shape[1]
    sent_delta = select_slots(full_delta.reshape(tb_dev, TBLK, full_width))
    sent_grad = select_slots(full_grad.reshape(tb_dev, TBLK, full_width))
    got_delta, got_grad = (
        lax.all_to_all(sent_delta, "tok", split_axis=0, concat_axis=0, tiled=True),
        lax.all_to_all(sent_grad, "tok", split_axis=0, concat_axis=0, tiled=True),
    )
    preactivation = jnp.einsum(
        "kstd,dc->kstc", got_delta, encoder, preferred_element_type=jnp.float32
    )
    gradient_inner_product = jnp.einsum(
        "kstd,cd->kstc", got_grad, decoder, preferred_element_type=jnp.float32
    )
    activation_value = jnp.maximum(preactivation + encoder_offset_bias, 0.0) * padded_output
    every_token_rows = tok_dev * tok_count
    scores = jnp.sum(activation_value * gradient_inner_product, axis=(0, 1, 2)) / math.sqrt(
        every_token_rows / 8
    )
    activation_half_precision = activation_value.astype(jnp.bfloat16)
    pieces_out = jnp.einsum(
        "fazg,gh->fazh", activation_half_precision, decoder, preferred_element_type=jnp.float32
    ).astype(jnp.bfloat16)
    returned = lax.all_to_all(pieces_out, "tok", split_axis=0, concat_axis=0, tiled=True)
    source_sums = jnp.einsum(
        "ksb,kstd->btd", chooser, returned, preferred_element_type=jnp.float32
    ).reshape(tok_dev, -1)
    shared = lax.psum_scatter(
        source_sums.astype(jnp.bfloat16), "lat", scatter_dimension=1, tiled=True
    )
    summed = lax.psum(shared, "pair").astype(jnp.float32)
    return ((summed + dec_bias).astype(jnp.bfloat16), scores)


MESH = pl.DeviceIdType.MESH
F32 = jnp.float32
BF16 = jnp.bfloat16
SLOT_ROWS = MOST * TBLK


def remote(src, dst, send_sem, recv_sem, device):
    return pltpu.make_async_remote_copy(
        src_ref=src,
        dst_ref=dst,
        send_sem=send_sem,
        recv_sem=recv_sem,
        device_id=device,
        device_id_type=MESH,
    )


def kernel(
    PAIR,
    LAT,
    TOK,
    residual,
    matches,
    grad,
    act,
    encoder,
    enc_bias,
    decoder,
    dec_bias,
    out,
    scores,
    win,
    match_all,
    part_out,
    part_in,
    own_delta,
    delta,
    grad_all,
    choose,
    choose_own,
    put,
    sent_delta,
    sent_grad,
    got_delta,
    got_grad,
    fire,
    pieces,
    back,
    enc_v,
    dec_v,
    local_sem,
    win_sem,
    match_send,
    match_recv,
    part_sem,
    grad_send,
    grad_recv,
    sd_send,
    sd_recv,
    sg_send,
    sg_recv,
    pc_send,
    pc_recv,
    out_sem,
):
    p = lax.axis_index("pair")
    l = lax.axis_index("lat")
    t = lax.axis_index("tok")
    rows, width = residual.shape
    half = width // PAIR
    group = PAIR * LAT
    j = p * LAT + l
    other = 1 - p
    tokens = rows * TOK
    has_left, has_right = t > 0, t < TOK - 1
    my_cols = pl.ds(pl.multiple_of(p * half, half), half)
    other_cols = pl.ds(pl.multiple_of(other * half, half), half)
    fc = l * PAIR + p

    peers = []
    for o in range(1, group):
        q = lax.rem(j + o, group)
        peers.append((q, q // LAT, lax.rem(q, LAT)))

    local = [
        pltpu.make_async_copy(residual.at[:, my_cols], win.at[p], local_sem.at[0]),
        pltpu.make_async_copy(grad.at[:, my_cols], grad_all.at[t], local_sem.at[1]),
        pltpu.make_async_copy(encoder, enc_v, local_sem.at[2]),
        pltpu.make_async_copy(decoder, dec_v, local_sem.at[3]),
    ]
    for copy in local:
        copy.start()

    barrier = pltpu.get_barrier_semaphore()
    for _, qp, ql in peers:
        pl.semaphore_signal(barrier, inc=1, device_id=(qp, ql, t), device_id_type=MESH)
    for step in range(1, TOK):
        where = lax.rem(t + step, TOK)
        for q in range(group):
            pl.semaphore_signal(
                barrier, inc=1, device_id=(q // LAT, q % LAT, where), device_id_type=MESH
            )

    n_sel = group * SLOT_ROWS
    r_id = lax.broadcasted_iota(jnp.int32, (n_sel, rows), 0)
    c_id = lax.broadcasted_iota(jnp.int32, (n_sel, rows), 1)
    first_of = (r_id // SLOT_ROWS) * TOK
    slot_of = lax.rem(r_id // TBLK, MOST).astype(F32)
    same_row = lax.rem(r_id, TBLK) == lax.rem(c_id, TBLK)
    u_r = lax.broadcasted_iota(jnp.int32, (rows, rows), 0)
    u_c = lax.broadcasted_iota(jnp.int32, (rows, rows), 1)
    before = jnp.where((u_r // TBLK < u_c // TBLK) & (lax.rem(u_r, TBLK) == 0), 1.0, 0.0).astype(BF16)

    def chosen(shard, plane):
        listed = jnp.zeros((n_sel, rows), F32)
        cols = pl.ds(pl.multiple_of(shard * rows, rows), rows)
        for a in range(act.shape[0]):
            listed = listed + jnp.where(act[a : a + 1, cols] == first_of + plane, 1.0, 0.0)
        rank = jnp.dot(listed.astype(BF16), before, preferred_element_type=F32)
        return jnp.where(same_row & (rank == slot_of), listed, 0.0)

    for s in range(TOK):
        choose[s] = chosen(s, t).astype(BF16)
        own = chosen(t, s)
        choose_own[s] = own.astype(BF16)
        put[s] = own.T.astype(BF16)

    pl.semaphore_wait(barrier, group * TOK - 1)

    match_all[p * 2] = matches[...]
    m_partner = remote(
        matches, match_all.at[p * 2], match_send.at[0], match_recv.at[p, 0], (other, l, t)
    )
    m_partner.start()
    m_left = [
        remote(matches, match_all.at[p * 2 + 1], match_send.at[1 + c], match_recv.at[p, 1], (c, l, t - 1))
        for c in range(PAIR)
    ]

    @pl.when(has_left)
    def _():
        for copy in m_left:
            copy.start()

    w_copy = remote(residual.at[:, other_cols], win.at[p], win_sem.at[0], win_sem.at[1], (other, l, t))
    w_copy.start()

    g_right = remote(grad.at[:, my_cols], grad_all.at[t], grad_send.at[t, 0], grad_recv.at[t], (p, l, t + 1))
    g_left = remote(grad.at[:, my_cols], grad_all.at[t], grad_send.at[t, 1], grad_recv.at[t], (p, l, t - 1))

    @pl.when(has_right)
    def _():
        g_right.start()

    @pl.when(has_left)
    def _():
        g_left.start()

    def pass_on(buf, send, recv, s):
        right = remote(buf.at[s], buf.at[s], send.at[s, 0], recv.at[s], (p, l, t + 1))
        left = remote(buf.at[s], buf.at[s], send.at[s, 1], recv.at[s], (p, l, t - 1))
        return right, left

    def order(i):
        m = jnp.minimum(t, TOK - 1 - t)
        d = (i + 1) // 2
        near = jnp.where(lax.rem(i, 2) == 1, t - d, t + d)
        far = jnp.where(t < TOK - 1 - t, t + (i - m), t - (i - m))
        return jnp.where(i <= 2 * m, near, far)

    def spread(i, buf, send, recv, sent, got, s_send, s_recv, first):
        s = order(i)
        right, left = pass_on(buf, send, recv, s)

        @pl.when(s != t)
        def _():
            right.wait_recv()

        own_goes = 0 if first else 1

        @pl.when(has_right & (s + own_goes <= t))
        def _():
            right.start()

        @pl.when(has_left & (s - own_goes >= t))
        def _():
            left.start()

        sent[s] = (
            jnp.dot(choose[s], buf[s], preferred_element_type=F32)
            .astype(BF16)
            .reshape(group, SLOT_ROWS, half)
        )
        for q, qp, ql in peers:
            remote(sent.at[s, q], got.at[fc, s], s_send.at[s, q], s_recv.at[fc, s], (qp, ql, t)).start()
        got[fc, s] = sent[s, j]

    def arrive(got, s_recv, s):
        for q, qp, ql in peers:
            qf = ql * PAIR + qp
            remote(got.at[qf, s], got.at[qf, s], s_recv.at[qf, s], s_recv.at[qf, s], (qp, ql, t)).wait_recv()

    def encode(i):
        s = order(i)
        arrive(got_delta, sd_recv, s)

        @pl.when(s != t)
        def _():
            remote(got_delta.at[fc, s], got_delta.at[fc, s], sd_recv.at[fc, s], sd_recv.at[fc, s], (p, l, s)).wait_recv()

        pre = jnp.zeros((SLOT_ROWS, enc_v.shape[1]), F32)
        for c in range(group):
            pre = pre + jnp.dot(
                got_delta[c, s], enc_v[c * half : (c + 1) * half, :], preferred_element_type=F32
            )
        firing = jnp.maximum(pre + enc_bias[...], 0.0)
        fire[s] = firing
        lean = firing.astype(BF16)
        for c in range(group):
            pieces[s, c] = jnp.dot(
                lean, dec_v[:, c * half : (c + 1) * half], preferred_element_type=F32
            ).astype(BF16)
        for q, qp, ql in peers:
            remote(
                pieces.at[s, ql * PAIR + qp], back.at[t, j], pc_send.at[s, q], pc_recv.at[t, j], (qp, ql, s)
            ).start()

        @pl.when(s != t)
        def _():
            remote(pieces.at[s, fc], back.at[t, j], pc_send.at[s, j], pc_recv.at[t, j], (p, l, s)).start()

    def spread_grad(i):
        spread(i, grad_all, grad_send, grad_recv, sent_grad, got_grad, sg_send, sg_recv, False)

    local[1].wait()
    spread_grad(0)
    m_recv = remote(matches, match_all.at[other * 2], match_send.at[0], match_recv.at[other, 0], (other, l, t))
    m_recv.wait_recv()
    local[0].wait()
    w_recv = remote(residual.at[:, other_cols], win.at[other], win_sem.at[0], win_sem.at[1], (other, l, t))
    w_recv.wait_recv()
    row_id = lax.broadcasted_iota(jnp.int32, (rows, rows), 0) + t * rows

    def matched(which):
        total = None
        for model, sign in ((0, -1.0), (1, 1.0)):
            hit = jnp.where(match_all[model * 2 + which] == row_id, sign, 0.0)
            term = jnp.dot(hit.T.astype(BF16), win[model], preferred_element_type=F32)
            total = term if total is None else total + term
        return total

    p_copy = remote(part_out, part_in, part_sem.at[0], part_sem.at[1], (p, l, t + 1))

    @pl.when(has_right)
    def _():
        for model in range(2):
            remote(
                matches, match_all.at[model * 2 + 1], match_send.at[0], match_recv.at[model, 1], (other, l, t)
            ).wait_recv()
        part_out[...] = matched(1).astype(BF16)
        p_copy.start()

    own_delta[...] = matched(0)
    if TOK > 1:
        spread_grad(1)

    @pl.when(has_left)
    def _():
        p_copy.wait_recv()
        own_delta[...] += part_in[...].astype(F32)

    delta[...] = own_delta[...].astype(BF16)

    def send_delta(k, carry):
        s = order(k)
        sent_delta[s] = (
            jnp.dot(choose_own[s], delta[...], preferred_element_type=F32)
            .astype(BF16)
            .reshape(group, SLOT_ROWS, half)
        )
        for q, qp, ql in peers:
            remote(sent_delta.at[s, q], got_delta.at[fc, t], sd_send.at[s, q], sd_recv.at[fc, t], (qp, ql, s)).start()

        @pl.when(s != t)
        def _():
            remote(sent_delta.at[s, j], got_delta.at[fc, t], sd_send.at[s, j], sd_recv.at[fc, t], (p, l, s)).start()

        return carry

    lax.fori_loop(0, TOK, send_delta, 0)
    got_delta[fc, t] = sent_delta[t, j]
    if TOK > 2:
        spread_grad(2)
    local[2].wait()
    local[3].wait()

    def step(i, carry):
        encode(i)
        return carry

    lax.fori_loop(0, TOK - 1, step, 0)
    for i in range(3, TOK):
        spread_grad(i)
    encode(TOK - 1)
    back[t, j] = pieces[t, fc]

    own_delta[...] = jnp.zeros_like(own_delta)

    def combine(i, carry):
        s = order(i)
        for q, qp, ql in peers:
            remote(back.at[s, q], back.at[s, q], pc_recv.at[s, q], pc_recv.at[s, q], (qp, ql, s)).wait_recv()

        @pl.when(s != t)
        def _():
            remote(back.at[s, j], back.at[s, j], pc_recv.at[s, j], pc_recv.at[s, j], (p, l, s)).wait_recv()

        own_delta[...] += jnp.dot(put[s], back[s].reshape(n_sel, half), preferred_element_type=F32)
        return carry

    lax.fori_loop(0, TOK, combine, 0)
    out[:, my_cols] = (own_delta[...] + dec_bias[:, my_cols]).astype(BF16)
    o_copy = remote(out.at[:, my_cols], out.at[:, my_cols], out_sem.at[0], out_sem.at[1], (other, l, t))
    o_copy.start()

    def arrive_grad(s, carry):
        arrive(got_grad, sg_recv, s)
        return carry

    lax.fori_loop(0, TOK, arrive_grad, 0)
    inner = jnp.zeros((TOK * SLOT_ROWS, enc_v.shape[1]), F32)
    for c in range(group):
        inner = inner + lax.dot_general(
            got_grad[c].reshape(TOK * SLOT_ROWS, half),
            dec_v[:, c * half : (c + 1) * half],
            (((1,), (1,)), ((), ())),
            preferred_element_type=F32,
        )

    total = jnp.zeros((1, enc_v.shape[1]), F32)
    heads = lax.rem(lax.broadcasted_iota(jnp.int32, (1, rows), 1), TBLK) == 0
    slot = (lax.broadcasted_iota(jnp.int32, (SLOT_ROWS, 1), 0) // TBLK).astype(F32)
    for s in range(TOK):
        mine = jnp.zeros((1, rows), F32)
        for a in range(act.shape[0]):
            mine = mine + jnp.where(act[a : a + 1, s * rows : (s + 1) * rows] == j * TOK + t, 1.0, 0.0)
        count = jnp.sum(jnp.where(heads, mine, 0.0), axis=1, keepdims=True)
        used = jnp.where(slot < count, fire[s], 0.0)
        total = total + jnp.sum(
            used * inner[s * SLOT_ROWS : (s + 1) * SLOT_ROWS], axis=0, keepdims=True
        )
    scores[...] = total / math.sqrt(tokens / TBLK)

    m_partner.wait_send()
    w_copy.wait_send()

    @pl.when(has_left)
    def _():
        for copy in m_left:
            copy.wait_send()

    @pl.when(has_right)
    def _():
        p_copy.wait_send()

    def drain(s, carry):
        right, left = pass_on(grad_all, grad_send, grad_recv, s)

        @pl.when(has_right & (s <= t))
        def _():
            right.wait_send()

        @pl.when(has_left & (s >= t))
        def _():
            left.wait_send()

        for q, qp, ql in peers:
            remote(sent_delta.at[s, q], got_delta.at[fc, s], sd_send.at[s, q], sd_recv.at[fc, s], (qp, ql, t)).wait_send()
            remote(sent_grad.at[s, q], got_grad.at[fc, s], sg_send.at[s, q], sg_recv.at[fc, s], (qp, ql, t)).wait_send()
            remote(pieces.at[s, q], back.at[s, j], pc_send.at[s, q], pc_recv.at[s, j], (qp, ql, t)).wait_send()

        @pl.when(s != t)
        def _():
            remote(sent_delta.at[s, j], got_delta.at[fc, s], sd_send.at[s, j], sd_recv.at[fc, s], (p, l, s)).wait_send()
            remote(pieces.at[s, j], back.at[s, j], pc_send.at[s, j], pc_recv.at[s, j], (p, l, s)).wait_send()

        return carry

    lax.fori_loop(0, TOK, drain, 0)
    o_copy.wait_send()
    remote(out.at[:, other_cols], out.at[:, other_cols], out_sem.at[0], out_sem.at[1], (other, l, t)).wait_recv()


def fused(
    residual, matches, kl_grad, active_blocks, encoder, encoder_offset_bias, decoder, dec_bias
):
    pair, lat, tok = (lax.axis_size(a) for a in ("pair", "lat", "tok"))
    _, rows, width = residual.shape
    half = width // pair
    group = pair * lat
    lats = encoder.shape[1]
    depth = encoder.shape[0]
    act = jnp.repeat(active_blocks.T, TBLK, axis=1)
    vmem = pl.BlockSpec(memory_space=pltpu.VMEM)
    hbm = pl.BlockSpec(memory_space=pltpu.HBM)
    dma = pltpu.SemaphoreType.DMA
    slots = (SLOT_ROWS, half)
    recon, scores = pl.pallas_call(
        functools.partial(kernel, pair, lat, tok),
        out_shape=(
            jax.ShapeDtypeStruct((rows, width), BF16),
            jax.ShapeDtypeStruct((1, lats), F32),
        ),
        in_specs=[hbm, vmem, hbm, vmem, hbm, vmem, hbm, vmem],
        out_specs=(vmem, vmem),
        scratch_shapes=[
            pltpu.VMEM((2, rows, half), BF16),
            pltpu.VMEM((4, 1, rows), jnp.int32),
            pltpu.VMEM((rows, half), BF16),
            pltpu.VMEM((rows, half), BF16),
            pltpu.VMEM((rows, half), F32),
            pltpu.VMEM((rows, half), BF16),
            pltpu.VMEM((tok, rows, half), BF16),
            pltpu.VMEM((tok, group * SLOT_ROWS, rows), BF16),
            pltpu.VMEM((tok, group * SLOT_ROWS, rows), BF16),
            pltpu.VMEM((tok, rows, group * SLOT_ROWS), BF16),
            pltpu.VMEM((tok, group) + slots, BF16),
            pltpu.VMEM((tok, group) + slots, BF16),
            pltpu.VMEM((group, tok) + slots, BF16),
            pltpu.VMEM((group, tok) + slots, BF16),
            pltpu.VMEM((tok, SLOT_ROWS, lats), F32),
            pltpu.VMEM((tok, group) + slots, BF16),
            pltpu.VMEM((tok, group) + slots, BF16),
            pltpu.VMEM((depth, lats), BF16),
            pltpu.VMEM((lats, depth), BF16),
            dma((4,)),
            dma((2,)),
            dma((3,)),
            dma((2, 2)),
            dma((2,)),
            dma((tok, 2)),
            dma((tok,)),
            dma((tok, group)),
            dma((group, tok)),
            dma((tok, group)),
            dma((group, tok)),
            dma((tok, group)),
            dma((tok, group)),
            dma((2,)),
        ],
        compiler_params=pltpu.CompilerParams(
            collective_id=0, has_side_effects=True, vmem_limit_bytes=67_000_000
        ),
    )(
        residual[0],
        matches,
        kl_grad,
        act,
        encoder,
        encoder_offset_bias[None],
        decoder,
        dec_bias[None],
    )
    return recon, scores[0]


def solution(mesh):
    placed = (
        P("pair", "tok", "lat"),
        P("pair", "tok"),
        P("tok", "lat"),
        P(),
        P(None, ("pair", "lat", "tok")),
        P(("pair", "lat", "tok")),
        P(("pair", "lat", "tok"), None),
        P("lat"),
    )


    def body(*args):
        residual = args[0]
        half = residual.shape[2] // mesh.shape["pair"]
        fits = mesh.shape["pair"] == 2 and residual.shape[2] % 2 == 0 and half % 128 == 0
        return (fused if fits else shards)(*args)

    return jax.shard_map(
        body,
        mesh=mesh,
        in_specs=placed,
        out_specs=(P("tok", "lat"), P(("pair", "lat", "tok"))),
        check_vma=False,
    )
```

```python
import functools
import math

import jax
import jax.numpy as jnp
from jax import lax
from jax.experimental import pallas as pl
from jax.experimental.pallas import tpu as pltpu
from jax.sharding import PartitionSpec as P

TBLK = 8
MOST = 2


def passed_along(x, axis, by):
    devices = lax.axis_size(axis)
    pairs = [(i, i + by) for i in range(devices) if 0 <= i + by < devices]
    return lax.ppermute(x, axis, pairs)


def from_partner(x, axis, bit):
    return lax.ppermute(x, axis, [(i, i ^ 1 << bit) for i in range(lax.axis_size(axis))])


def slot_table(my_lists, targets, slot_ids):
    listed = jnp.any(my_lists[:, :, None] == targets[None, None, :], axis=1).astype(jnp.int32)
    ranking = jnp.cumsum(listed, axis=0) - listed
    return (listed.T[:, None, :] * (ranking.T[:, None, :] == slot_ids[None, :, None])).astype(
        jnp.bfloat16
    )


def shards(
    residual, matches, kl_grad, active_blocks, encoder, encoder_offset_bias, decoder, dec_bias
):
    tok_dev = residual.shape[1]
    tok_count = lax.axis_size("tok")
    lat_count = lax.axis_size("lat")
    tok_here = lax.axis_index("tok")
    own_rows = residual[0]
    earlier = passed_along(own_rows, "tok", 1)
    window = jnp.concatenate([earlier, own_rows], axis=0)
    first_row = (tok_here - 1) * tok_dev
    local_index = matches[0] - first_row
    matched = jnp.take(window, local_index, axis=0)
    partner = from_partner(matched, "pair", 0)
    is_chat = lax.axis_index("pair") == 1
    chat_rows = jnp.where(is_chat, matched, partner)
    base_rows = jnp.where(is_chat, partner, matched)
    delta_rows = (chat_rows.astype(jnp.float32) - base_rows.astype(jnp.float32)).astype(
        jnp.bfloat16
    )
    tb_dev = tok_dev // TBLK
    pair_base = lax.axis_index("pair") * lat_count
    row_base = (pair_base + lax.axis_index("lat")) * tok_count
    my_block = row_base + tok_here
    my_lists = lax.dynamic_slice_in_dim(active_blocks, tok_here * tb_dev, tb_dev, 0)
    slot_ids = jnp.arange(MOST, dtype=jnp.int32)
    targets = row_base + jnp.arange(tok_count, dtype=jnp.int32)
    chooser = slot_table(my_lists, targets, slot_ids)
    mine_listed = jnp.any(active_blocks == my_block, axis=1).astype(jnp.int32)
    counts = jnp.sum(mine_listed.reshape(tok_count, tb_dev), axis=1)
    padded_output = (slot_ids[None, :] < counts[:, None]).astype(jnp.float32)[:, :, None, None]

    def select_slots(blocks):
        return jnp.einsum(
            "ksb,btd->kstd", chooser, blocks, preferred_element_type=jnp.float32
        ).astype(jnp.bfloat16)

    full_delta, full_grad = (
        lax.all_gather(delta_rows, "lat", axis=1, tiled=True),
        lax.all_gather(kl_grad, "lat", axis=1, tiled=True),
    )
    full_width = full_delta.shape[1]
    sent_delta = select_slots(full_delta.reshape(tb_dev, TBLK, full_width))
    sent_grad = select_slots(full_grad.reshape(tb_dev, TBLK, full_width))
    got_delta, got_grad = (
        lax.all_to_all(sent_delta, "tok", split_axis=0, concat_axis=0, tiled=True),
        lax.all_to_all(sent_grad, "tok", split_axis=0, concat_axis=0, tiled=True),
    )
    preactivation = jnp.einsum(
        "kstd,dc->kstc", got_delta, encoder, preferred_element_type=jnp.float32
    )
    gradient_inner_product = jnp.einsum(
        "kstd,cd->kstc", got_grad, decoder, preferred_element_type=jnp.float32
    )
    activation_value = jnp.maximum(preactivation + encoder_offset_bias, 0.0) * padded_output
    every_token_rows = tok_dev * tok_count
    scores = jnp.sum(activation_value * gradient_inner_product, axis=(0, 1, 2)) / math.sqrt(
        every_token_rows / 8
    )
    activation_half_precision = activation_value.astype(jnp.bfloat16)
    pieces_out = jnp.einsum(
        "fazg,gh->fazh", activation_half_precision, decoder, preferred_element_type=jnp.float32
    ).astype(jnp.bfloat16)
    returned = lax.all_to_all(pieces_out, "tok", split_axis=0, concat_axis=0, tiled=True)
    source_sums = jnp.einsum(
        "ksb,kstd->btd", chooser, returned, preferred_element_type=jnp.float32
    ).reshape(tok_dev, -1)
    shared = lax.psum_scatter(
        source_sums.astype(jnp.bfloat16), "lat", scatter_dimension=1, tiled=True
    )
    summed = lax.psum(shared, "pair").astype(jnp.float32)
    return ((summed + dec_bias).astype(jnp.bfloat16), scores)


MESH = pl.DeviceIdType.MESH
F32 = jnp.float32
BF16 = jnp.bfloat16
SLOT_ROWS = MOST * TBLK


def remote(src, dst, send_sem, recv_sem, device):
    return pltpu.make_async_remote_copy(
        src_ref=src,
        dst_ref=dst,
        send_sem=send_sem,
        recv_sem=recv_sem,
        device_id=device,
        device_id_type=MESH,
    )


def kernel(
    PAIR,
    LAT,
    TOK,
    residual,
    matches,
    grad,
    act,
    encoder,
    enc_bias,
    decoder,
    dec_bias,
    out,
    scores,
    win,
    match_all,
    part_out,
    part_in,
    own_delta,
    delta,
    grad_all,
    choose,
    choose_own,
    put,
    sent_delta,
    sent_grad,
    got_delta,
    got_grad,
    fire,
    pieces,
    back,
    enc_v,
    dec_v,
    local_sem,
    win_sem,
    match_send,
    match_recv,
    part_sem,
    grad_send,
    grad_recv,
    sd_send,
    sd_recv,
    sg_send,
    sg_recv,
    pc_send,
    pc_recv,
    out_sem,
):
    p = lax.axis_index("pair")
    l = lax.axis_index("lat")
    t = lax.axis_index("tok")
    rows, width = residual.shape
    half = width // PAIR
    group = PAIR * LAT
    j = p * LAT + l
    other = 1 - p
    tokens = rows * TOK
    has_left, has_right = t > 0, t < TOK - 1
    my_cols = pl.ds(pl.multiple_of(p * half, half), half)
    other_cols = pl.ds(pl.multiple_of(other * half, half), half)
    fc = l * PAIR + p

    peers = []
    for o in range(1, group):
        q = lax.rem(j + o, group)
        peers.append((q, q // LAT, lax.rem(q, LAT)))

    local = [
        pltpu.make_async_copy(residual.at[:, my_cols], win.at[p], local_sem.at[0]),
        pltpu.make_async_copy(grad.at[:, my_cols], grad_all.at[t], local_sem.at[1]),
        pltpu.make_async_copy(encoder, enc_v, local_sem.at[2]),
        pltpu.make_async_copy(decoder, dec_v, local_sem.at[3]),
    ]
    for copy in local:
        copy.start()

    barrier = pltpu.get_barrier_semaphore()
    for _, qp, ql in peers:
        pl.semaphore_signal(barrier, inc=1, device_id=(qp, ql, t), device_id_type=MESH)
    for step in range(1, TOK):
        where = lax.rem(t + step, TOK)
        for q in range(group):
            pl.semaphore_signal(
                barrier, inc=1, device_id=(q // LAT, q % LAT, where), device_id_type=MESH
            )

    n_sel = group * SLOT_ROWS
    r_id = lax.broadcasted_iota(jnp.int32, (n_sel, rows), 0)
    c_id = lax.broadcasted_iota(jnp.int32, (n_sel, rows), 1)
    first_of = (r_id // SLOT_ROWS) * TOK
    slot_of = lax.rem(r_id // TBLK, MOST).astype(F32)
    same_row = lax.rem(r_id, TBLK) == lax.rem(c_id, TBLK)
    u_r = lax.broadcasted_iota(jnp.int32, (rows, rows), 0)
    u_c = lax.broadcasted_iota(jnp.int32, (rows, rows), 1)
    before = jnp.where((u_r // TBLK < u_c // TBLK) & (lax.rem(u_r, TBLK) == 0), 1.0, 0.0).astype(BF16)

    def chosen(shard, plane):
        listed = jnp.zeros((n_sel, rows), F32)
        cols = pl.ds(pl.multiple_of(shard * rows, rows), rows)
        for a in range(act.shape[0]):
            listed = listed + jnp.where(act[a : a + 1, cols] == first_of + plane, 1.0, 0.0)
        rank = jnp.dot(listed.astype(BF16), before, preferred_element_type=F32)
        return jnp.where(same_row & (rank == slot_of), listed, 0.0)

    for s in range(TOK):
        choose[s] = chosen(s, t).astype(BF16)
        own = chosen(t, s)
        choose_own[s] = own.astype(BF16)
        put[s] = own.T.astype(BF16)

    pl.semaphore_wait(barrier, group * TOK - 1)

    match_all[p * 2] = matches[...]
    m_partner = remote(
        matches, match_all.at[p * 2], match_send.at[0], match_recv.at[p, 0], (other, l, t)
    )
    m_partner.start()
    m_left = [
        remote(matches, match_all.at[p * 2 + 1], match_send.at[1 + c], match_recv.at[p, 1], (c, l, t - 1))
        for c in range(PAIR)
    ]

    @pl.when(has_left)
    def _():
        for copy in m_left:
            copy.start()

    w_copy = remote(residual.at[:, other_cols], win.at[p], win_sem.at[0], win_sem.at[1], (other, l, t))
    w_copy.start()

    g_right = remote(grad.at[:, my_cols], grad_all.at[t], grad_send.at[t, 0], grad_recv.at[t], (p, l, t + 1))
    g_left = remote(grad.at[:, my_cols], grad_all.at[t], grad_send.at[t, 1], grad_recv.at[t], (p, l, t - 1))

    @pl.when(has_right)
    def _():
        g_right.start()

    @pl.when(has_left)
    def _():
        g_left.start()

    def pass_on(buf, send, recv, s):
        right = remote(buf.at[s], buf.at[s], send.at[s, 0], recv.at[s], (p, l, t + 1))
        left = remote(buf.at[s], buf.at[s], send.at[s, 1], recv.at[s], (p, l, t - 1))
        return right, left

    def order(i):
        m = jnp.minimum(t, TOK - 1 - t)
        d = (i + 1) // 2
        near = jnp.where(lax.rem(i, 2) == 1, t - d, t + d)
        far = jnp.where(t < TOK - 1 - t, t + (i - m), t - (i - m))
        return jnp.where(i <= 2 * m, near, far)

    def spread(i, buf, send, recv, sent, got, s_send, s_recv, first):
        s = order(i)
        right, left = pass_on(buf, send, recv, s)

        @pl.when(s != t)
        def _():
            right.wait_recv()

        own_goes = 0 if first else 1

        @pl.when(has_right & (s + own_goes <= t))
        def _():
            right.start()

        @pl.when(has_left & (s - own_goes >= t))
        def _():
            left.start()

        sent[s] = (
            jnp.dot(choose[s], buf[s], preferred_element_type=F32)
            .astype(BF16)
            .reshape(group, SLOT_ROWS, half)
        )
        for q, qp, ql in peers:
            remote(sent.at[s, q], got.at[fc, s], s_send.at[s, q], s_recv.at[fc, s], (qp, ql, t)).start()
        got[fc, s] = sent[s, j]

    def arrive(got, s_recv, s):
        for q, qp, ql in peers:
            qf = ql * PAIR + qp
            remote(got.at[qf, s], got.at[qf, s], s_recv.at[qf, s], s_recv.at[qf, s], (qp, ql, t)).wait_recv()

    def encode(i):
        s = order(i)
        arrive(got_delta, sd_recv, s)

        @pl.when(s != t)
        def _():
            remote(got_delta.at[fc, s], got_delta.at[fc, s], sd_recv.at[fc, s], sd_recv.at[fc, s], (p, l, s)).wait_recv()

        pre = jnp.zeros((SLOT_ROWS, enc_v.shape[1]), F32)
        for c in range(group):
            pre = pre + jnp.dot(
                got_delta[c, s], enc_v[c * half : (c + 1) * half, :], preferred_element_type=F32
            )
        firing = jnp.maximum(pre + enc_bias[...], 0.0)
        fire[s] = firing
        lean = firing.astype(BF16)
        for c in range(group):
            pieces[s, c] = jnp.dot(
                lean, dec_v[:, c * half : (c + 1) * half], preferred_element_type=F32
            ).astype(BF16)
        for q, qp, ql in peers:
            remote(
                pieces.at[s, ql * PAIR + qp], back.at[t, j], pc_send.at[s, q], pc_recv.at[t, j], (qp, ql, s)
            ).start()

        @pl.when(s != t)
        def _():
            remote(pieces.at[s, fc], back.at[t, j], pc_send.at[s, j], pc_recv.at[t, j], (p, l, s)).start()

    def spread_grad(i):
        spread(i, grad_all, grad_send, grad_recv, sent_grad, got_grad, sg_send, sg_recv, False)

    local[1].wait()
    spread_grad(0)
    m_recv = remote(matches, match_all.at[other * 2], match_send.at[0], match_recv.at[other, 0], (other, l, t))
    m_recv.wait_recv()
    local[0].wait()
    w_recv = remote(residual.at[:, other_cols], win.at[other], win_sem.at[0], win_sem.at[1], (other, l, t))
    w_recv.wait_recv()
    row_id = lax.broadcasted_iota(jnp.int32, (rows, rows), 0) + t * rows

    def matched(which):
        total = None
        for model, sign in ((0, -1.0), (1, 1.0)):
            hit = jnp.where(match_all[model * 2 + which] == row_id, sign, 0.0)
            term = jnp.dot(hit.T.astype(BF16), win[model], preferred_element_type=F32)
            total = term if total is None else total + term
        return total

    p_copy = remote(part_out, part_in, part_sem.at[0], part_sem.at[1], (p, l, t + 1))

    @pl.when(has_right)
    def _():
        for model in range(2):
            remote(
                matches, match_all.at[model * 2 + 1], match_send.at[0], match_recv.at[model, 1], (other, l, t)
            ).wait_recv()
        part_out[...] = matched(1).astype(BF16)
        p_copy.start()

    own_delta[...] = matched(0)
    if TOK > 1:
        spread_grad(1)

    @pl.when(has_left)
    def _():
        p_copy.wait_recv()
        own_delta[...] += part_in[...].astype(F32)

    delta[...] = own_delta[...].astype(BF16)

    def send_delta(k, carry):
        s = order(k)
        sent_delta[s] = (
            jnp.dot(choose_own[s], delta[...], preferred_element_type=F32)
            .astype(BF16)
            .reshape(group, SLOT_ROWS, half)
        )
        for q, qp, ql in peers:
            remote(sent_delta.at[s, q], got_delta.at[fc, t], sd_send.at[s, q], sd_recv.at[fc, t], (qp, ql, s)).start()

        @pl.when(s != t)
        def _():
            remote(sent_delta.at[s, j], got_delta.at[fc, t], sd_send.at[s, j], sd_recv.at[fc, t], (p, l, s)).start()

        return carry

    lax.fori_loop(0, TOK, send_delta, 0)
    got_delta[fc, t] = sent_delta[t, j]
    if TOK > 2:
        spread_grad(2)
    local[2].wait()
    local[3].wait()

    def step(i, carry):
        encode(i)
        return carry

    lax.fori_loop(0, TOK - 1, step, 0)
    encode(TOK - 1)
    for i in range(3, TOK):
        spread_grad(i)
    back[t, j] = pieces[t, fc]

    own_delta[...] = jnp.zeros_like(own_delta)

    def combine(i, carry):
        s = order(i)
        for q, qp, ql in peers:
            remote(back.at[s, q], back.at[s, q], pc_recv.at[s, q], pc_recv.at[s, q], (qp, ql, s)).wait_recv()

        @pl.when(s != t)
        def _():
            remote(back.at[s, j], back.at[s, j], pc_recv.at[s, j], pc_recv.at[s, j], (p, l, s)).wait_recv()

        own_delta[...] += jnp.dot(put[s], back[s].reshape(n_sel, half), preferred_element_type=F32)
        return carry

    lax.fori_loop(0, TOK, combine, 0)
    out[:, my_cols] = (own_delta[...] + dec_bias[:, my_cols]).astype(BF16)
    o_copy = remote(out.at[:, my_cols], out.at[:, my_cols], out_sem.at[0], out_sem.at[1], (other, l, t))
    o_copy.start()

    def arrive_grad(s, carry):
        arrive(got_grad, sg_recv, s)
        return carry

    lax.fori_loop(0, TOK, arrive_grad, 0)
    inner = jnp.zeros((TOK * SLOT_ROWS, enc_v.shape[1]), F32)
    for c in range(group):
        inner = inner + lax.dot_general(
            got_grad[c].reshape(TOK * SLOT_ROWS, half),
            dec_v[:, c * half : (c + 1) * half],
            (((1,), (1,)), ((), ())),
            preferred_element_type=F32,
        )

    total = jnp.zeros((1, enc_v.shape[1]), F32)
    heads = lax.rem(lax.broadcasted_iota(jnp.int32, (1, rows), 1), TBLK) == 0
    slot = (lax.broadcasted_iota(jnp.int32, (SLOT_ROWS, 1), 0) // TBLK).astype(F32)
    for s in range(TOK):
        mine = jnp.zeros((1, rows), F32)
        for a in range(act.shape[0]):
            mine = mine + jnp.where(act[a : a + 1, s * rows : (s + 1) * rows] == j * TOK + t, 1.0, 0.0)
        count = jnp.sum(jnp.where(heads, mine, 0.0), axis=1, keepdims=True)
        used = jnp.where(slot < count, fire[s], 0.0)
        total = total + jnp.sum(
            used * inner[s * SLOT_ROWS : (s + 1) * SLOT_ROWS], axis=0, keepdims=True
        )
    scores[...] = total / math.sqrt(tokens / TBLK)

    m_partner.wait_send()
    w_copy.wait_send()

    @pl.when(has_left)
    def _():
        for copy in m_left:
            copy.wait_send()

    @pl.when(has_right)
    def _():
        p_copy.wait_send()

    def drain(s, carry):
        right, left = pass_on(grad_all, grad_send, grad_recv, s)

        @pl.when(has_right & (s <= t))
        def _():
            right.wait_send()

        @pl.when(has_left & (s >= t))
        def _():
            left.wait_send()

        for q, qp, ql in peers:
            remote(sent_delta.at[s, q], got_delta.at[fc, s], sd_send.at[s, q], sd_recv.at[fc, s], (qp, ql, t)).wait_send()
            remote(sent_grad.at[s, q], got_grad.at[fc, s], sg_send.at[s, q], sg_recv.at[fc, s], (qp, ql, t)).wait_send()
            remote(pieces.at[s, q], back.at[s, j], pc_send.at[s, q], pc_recv.at[s, j], (qp, ql, t)).wait_send()

        @pl.when(s != t)
        def _():
            remote(sent_delta.at[s, j], got_delta.at[fc, s], sd_send.at[s, j], sd_recv.at[fc, s], (p, l, s)).wait_send()
            remote(pieces.at[s, j], back.at[s, j], pc_send.at[s, j], pc_recv.at[s, j], (p, l, s)).wait_send()

        return carry

    lax.fori_loop(0, TOK, drain, 0)
    o_copy.wait_send()
    remote(out.at[:, other_cols], out.at[:, other_cols], out_sem.at[0], out_sem.at[1], (other, l, t)).wait_recv()


def fused(
    residual, matches, kl_grad, active_blocks, encoder, encoder_offset_bias, decoder, dec_bias
):
    pair, lat, tok = (lax.axis_size(a) for a in ("pair", "lat", "tok"))
    _, rows, width = residual.shape
    half = width // pair
    group = pair * lat
    lats = encoder.shape[1]
    depth = encoder.shape[0]
    act = jnp.repeat(active_blocks.T, TBLK, axis=1)
    vmem = pl.BlockSpec(memory_space=pltpu.VMEM)
    hbm = pl.BlockSpec(memory_space=pltpu.HBM)
    dma = pltpu.SemaphoreType.DMA
    slots = (SLOT_ROWS, half)
    recon, scores = pl.pallas_call(
        functools.partial(kernel, pair, lat, tok),
        out_shape=(
            jax.ShapeDtypeStruct((rows, width), BF16),
            jax.ShapeDtypeStruct((1, lats), F32),
        ),
        in_specs=[hbm, vmem, hbm, vmem, hbm, vmem, hbm, vmem],
        out_specs=(vmem, vmem),
        scratch_shapes=[
            pltpu.VMEM((2, rows, half), BF16),
            pltpu.VMEM((4, 1, rows), jnp.int32),
            pltpu.VMEM((rows, half), BF16),
            pltpu.VMEM((rows, half), BF16),
            pltpu.VMEM((rows, half), F32),
            pltpu.VMEM((rows, half), BF16),
            pltpu.VMEM((tok, rows, half), BF16),
            pltpu.VMEM((tok, group * SLOT_ROWS, rows), BF16),
            pltpu.VMEM((tok, group * SLOT_ROWS, rows), BF16),
            pltpu.VMEM((tok, rows, group * SLOT_ROWS), BF16),
            pltpu.VMEM((tok, group) + slots, BF16),
            pltpu.VMEM((tok, group) + slots, BF16),
            pltpu.VMEM((group, tok) + slots, BF16),
            pltpu.VMEM((group, tok) + slots, BF16),
            pltpu.VMEM((tok, SLOT_ROWS, lats), F32),
            pltpu.VMEM((tok, group) + slots, BF16),
            pltpu.VMEM((tok, group) + slots, BF16),
            pltpu.VMEM((depth, lats), BF16),
            pltpu.VMEM((lats, depth), BF16),
            dma((4,)),
            dma((2,)),
            dma((3,)),
            dma((2, 2)),
            dma((2,)),
            dma((tok, 2)),
            dma((tok,)),
            dma((tok, group)),
            dma((group, tok)),
            dma((tok, group)),
            dma((group, tok)),
            dma((tok, group)),
            dma((tok, group)),
            dma((2,)),
        ],
        compiler_params=pltpu.CompilerParams(
            collective_id=0, has_side_effects=True, vmem_limit_bytes=67_000_000
        ),
    )(
        residual[0],
        matches,
        kl_grad,
        act,
        encoder,
        encoder_offset_bias[None],
        decoder,
        dec_bias[None],
    )
    return recon, scores[0]


def solution(mesh):
    placed = (
        P("pair", "tok", "lat"),
        P("pair", "tok"),
        P("tok", "lat"),
        P(),
        P(None, ("pair", "lat", "tok")),
        P(("pair", "lat", "tok")),
        P(("pair", "lat", "tok"), None),
        P("lat"),
    )


    def body(*args):
        residual = args[0]
        half = residual.shape[2] // mesh.shape["pair"]
        fits = mesh.shape["pair"] == 2 and residual.shape[2] % 2 == 0 and half % 128 == 0
        return (fused if fits else shards)(*args)

    return jax.shard_map(
        body,
        mesh=mesh,
        in_specs=placed,
        out_specs=(P("tok", "lat"), P(("pair", "lat", "tok"))),
        check_vma=False,
    )
```
